256 devices in a mesh: row: 32 (over x, y, core), col: 8 (over z).
Axes of the slice: x: 4, y: 4, z: 8, core: 2. Of those that a mesh axis runs over, the one named last changes fastest.
Arguments:
- matrix: bfloat16 [65536, 8192], P('row', 'col'), may hold values from 0 to 1
- labels: int32 [65536, 1], P('row'), may hold values from 0 to 7
- root_rows: float32 [8, 65536], P(None, 'row'), may hold values from 0.2 to 1
- root_cols: float32 [8, 8192], P(None, 'col'), may hold values from 0.2 to 1
- child_rows: float32 [16, 65536], P(None, 'row'), may hold values from 0.2 to 1
- child_cols: float32 [128, 8192], P(None, 'col'), may hold values from 0.2 to 1
Outputs:
- root_w: float32 [8, 65536], P(None, 'row')
- root_h: float32 [8, 8192], P(None, 'col')
- child_w: float32 [16, 65536], P(None, 'row')
- child_h: float32 [128, 8192], P(None, 'col')
The draws below stay inside these ranges and needn't reach their ends.
Inputs may be any that keep to these rules, and one draw needn't show every extreme that they name: `labels`: every cluster 0 to 7 holds at least one node.
All inputs are finite; a program needn't handle non-finite values.
Results may differ from the reference program's by a relative error of at most 0.00035.
Values sent between devices are 32-bit elements; how exact they have to be, the bound alone decides.
A program may use at most 64 MiB of HBM per device.

```python
import jax
import jax.numpy as jnp
from jax import lax

BINS = 8192
K_ROOT = 8
K_CHILD = 16
CHILDREN = 8
ROOT_ITERS = 2
CHILD_ITERS = 3
NODES = 65536


def shard_levels(rng, shape, split, least, high):
    gain = 1.0
    for position, parts in split:
        heights = jax.random.uniform(jax.random.fold_in(jax.random.fold_in(rng, 6), position), (parts,), jnp.float32, least / len(split), high / len(split))
        gain = gain * jnp.repeat(jnp.exp(heights), shape[position] // parts).reshape((-1,) + (1,) * (len(shape) - 1 - position))
    return gain


def choose_distinct(own_key, rows, amount, top, lift):
    sequence = jax.random.permutation(jax.random.fold_in(own_key, 1), amount)
    boost = sequence
    for power in range(3):
        boost = boost * boost // amount
    boost = boost * lift // amount
    lots = jax.random.randint(jax.random.fold_in(own_key, 2), (rows, amount), 0, 4096) + boost
    holders = jax.random.permutation(jax.random.fold_in(own_key, 3), rows)[jnp.arange(amount) % rows]
    lots = jnp.where(jnp.arange(rows)[:, None] == holders[None, :], 1 << 14, lots)
    priority = lots * amount + jnp.arange(amount)
    return lax.top_k(priority.astype(jnp.int32), top)[1].astype(jnp.int32)


def setup_inputs(seed: int = 0) -> dict:
    seeds = jax.random.split(jax.random.key(seed), 7)
    return {
        "matrix": jnp.clip(1.0 * jax.random.uniform(seeds[0], (NODES, BINS), jnp.float32) ** shard_levels(seeds[0], (NODES, BINS), ((0, 32), (1, 8)), -0.2, 0.2), 0.0, 1.0).astype(jnp.bfloat16),
        "labels": choose_distinct(seeds[1], NODES, CHILDREN, 1, 2048),
        "root_rows": jnp.clip(0.2 + 0.8 * jax.random.uniform(seeds[2], (K_ROOT, NODES), jnp.float32) ** shard_levels(seeds[2], (K_ROOT, NODES), ((1, 32),), -0.2, 0.2), 0.2, 1.0),
        "root_cols": jnp.clip(0.2 + 0.8 * jax.random.uniform(seeds[3], (K_ROOT, BINS), jnp.float32) ** shard_levels(seeds[3], (K_ROOT, BINS), ((1, 8),), -0.2, 0.2), 0.2, 1.0),
        "child_rows": jnp.clip(0.2 + 0.8 * jax.random.uniform(seeds[4], (K_CHILD, NODES), jnp.float32) ** shard_levels(seeds[4], (K_CHILD, NODES), ((1, 32),), -0.2, 0.2), 0.2, 1.0),
        "child_cols": jnp.clip(0.2 + 0.8 * jax.random.uniform(seeds[5], (CHILDREN * K_CHILD, BINS), jnp.float32) ** shard_levels(seeds[5], (CHILDREN * K_CHILD, BINS), ((1, 8),), -0.2, 0.2), 0.2, 1.0),
    }


HIGH = lax.Precision.HIGHEST


def times_transpose(left_bf, matrix):
    return lax.dot_general(left_bf, matrix, (((1,), (1,)), ((), ())), preferred_element_type=jnp.float32)


def reference(matrix, labels, root_rows, root_cols, child_rows, child_cols):
    root_w = root_rows
    root_h = root_cols
    for iteration in range(ROOT_ITERS):
        numer_h = jnp.dot(root_w.astype(jnp.bfloat16), matrix, preferred_element_type=jnp.float32)
        gram_w = jnp.dot(root_w, root_w.T, precision=HIGH)
        root_h = root_h * numer_h / jnp.dot(gram_w, root_h, precision=HIGH)
        numer_w = times_transpose(root_h.astype(jnp.bfloat16), matrix)
        gram_h = jnp.dot(root_h, root_h.T, precision=HIGH)
        root_w = root_w * numer_w / jnp.dot(gram_h, root_w, precision=HIGH)
    member = (labels[:, 0][None, :] == jnp.arange(CHILDREN, dtype=jnp.int32)[:, None]).astype(jnp.float32)
    own_weight = jnp.sum(member * root_w, axis=0)
    child_w = child_rows * own_weight[None, :]
    child_h = child_cols * jnp.repeat(root_h, K_CHILD, axis=0)
    for iteration in range(CHILD_ITERS):
        spread = member[:, None, :] * child_w[None, :, :]
        spread_bf = spread.reshape(CHILDREN * K_CHILD, -1).astype(jnp.bfloat16)
        numer_ch = jnp.dot(spread_bf, matrix, preferred_element_type=jnp.float32)
        gram_c = jnp.einsum('cjr,ckr->cjk', spread, spread, precision=HIGH)
        blocks = child_h.reshape(CHILDREN, K_CHILD, -1)
        lower = jnp.einsum('cjk,ckn->cjn', gram_c, blocks, precision=HIGH).reshape(CHILDREN * K_CHILD, -1)
        child_h = child_h * numer_ch / lower
        full_rows = times_transpose(child_h.astype(jnp.bfloat16), matrix)
        numer_cw = jnp.sum(full_rows.reshape(CHILDREN, K_CHILD, -1) * member[:, None, :], axis=0)
        blocks = child_h.reshape(CHILDREN, K_CHILD, -1)
        hgram = jnp.einsum('cjn,ckn->cjk', blocks, blocks, precision=HIGH)
        lower_w = jnp.sum(jnp.einsum('cjk,kr->cjr', hgram, child_w, precision=HIGH) * member[:, None, :], axis=0)
        child_w = child_w * numer_cw / lower_w
    return root_w, root_h, child_w, child_h
```

```python
import functools

import jax
import jax.numpy as jnp
from jax import lax
from jax.experimental import pallas as pl
from jax.experimental.pallas import tpu as pltpu
from jax.sharding import PartitionSpec as P

MESH = pl.DeviceIdType.MESH
F32, BF16 = jnp.float32, jnp.bfloat16
K_ROOT, K_CHILD, CHILDREN = 8, 16, 8
ROOT_ITERS, CHILD_ITERS = 2, 3
TOTAL = CHILDREN * K_CHILD
NODES, BINS, HALF = 2048, 1024, 512
ZN, CHUNK = 8, 256
CHIPS = 16


def ring(d, n):
    return min(d, n - d)


XY = sorted(
    [(dx, dy) for dx in range(4) for dy in range(4) if dx or dy],
    key=lambda o: -(ring(o[0], 4) + ring(o[1], 4)),
)
XY_ARRIVAL = list(reversed(range(len(XY))))
Z_SEND = [4, 3, 5, 2, 6, 1, 7]
Z_ARRIVAL = [1, 7, 2, 6, 3, 5, 4]


def nn(a, b):
    return jnp.dot(a, b, preferred_element_type=F32)


def nt(a, b):
    return lax.dot_general(a, b, (((1,), (1,)), ((), ())), preferred_element_type=F32)


def parts(a):
    high = a.astype(BF16)
    return high, (a - high.astype(F32)).astype(BF16)


def gram3(high, low):
    return nt(high, high) + (nt(high, low) + nt(low, high))


def padded(gram):
    rows, cols = gram.shape
    return jnp.concatenate([gram, jnp.zeros((rows, 128 - cols), F32)], axis=1)


def small_product(gram, rows, count):
    total = gram[:, 0:1] * rows[0:1, :]
    for k in range(1, count):
        total = total + gram[:, k : k + 1] * rows[k : k + 1, :]
    return total


def kernel(
    x_hbm, lab_ref, rr_ref, rc_hbm, cr_ref, cc_hbm,
    o_rw, o_rh, o_cw, o_ch,
    xv, cc, lb, crv, rh, rw, cw, hb, hbb, acc, no, gacc,
    rxs, rxr, fr, zs_r, zr_r,
    nps, cxr, gxs, gxr, rss, rsr, zs_c, zr_c,
    in_sem, out_sem,
    s_rx, r_rx, s_fr, r_fr, s_rh, r_rh, s_zr, r_zr, s_rw, r_rw,
    s_cx, r_cx, s_rs, r_rs, s_ag, r_ag, s_re, r_re, s_zc, r_zc, s_cw, r_cw,
):
    row, z = lax.axis_index("row"), lax.axis_index("col")
    p, core = lax.div(row, 2), lax.rem(row, 2)
    x, y = lax.div(p, 4), lax.rem(p, 4)
    child = lax.div(p, 2)

    def chip(dx, dy):
        return lax.rem(x + dx + 4, 4) * 4 + lax.rem(y + dy + 4, 4)

    def xy_peer(o):
        return {"row": chip(*o) * 2 + core, "col": z}

    def z_at(d):
        return lax.rem(z + d + ZN, ZN)

    def z_peer(d):
        return {"row": row, "col": z_at(d)}

    partner = {"row": p * 2 + 1 - core, "col": z}
    pending = []

    def send(src, dst, ssem, rsem, device):
        copy = pltpu.make_async_remote_copy(
            src_ref=src, dst_ref=dst, send_sem=ssem, recv_sem=rsem,
            device_id=device, device_id_type=MESH,
        )
        copy.start()
        pending.append(copy)
        return copy

    def flush(keep):
        while len(pending) > keep:
            pending.pop(0).wait_send()

    loads = []
    for half in range(2):
        first = pl.multiple_of(HALF * (core if half == 0 else 1 - core), HALF)
        for i in range(4):
            rows = pl.ds(i * 512, 512)
            loads.append(
                pltpu.make_async_copy(
                    x_hbm.at[rows, pl.ds(first, HALF)], xv.at[half, rows], in_sem.at[half * 4 + i]
                )
            )
    own_cols = pl.ds(pl.multiple_of(HALF * core, HALF), HALF)
    other_cols = pl.ds(pl.multiple_of(HALF * (1 - core), HALF), HALF)
    load_cc = pltpu.make_async_copy(
        cc_hbm.at[pl.ds(pl.multiple_of(child * K_CHILD, 16), K_CHILD), own_cols], cc, in_sem.at[8]
    )
    load_rc = pltpu.make_async_copy(rc_hbm.at[:, own_cols], rh.at[0, 0], in_sem.at[9])
    for load in loads:
        load.start()
    load_rc.start()
    load_cc.start()

    barrier = pltpu.get_barrier_semaphore()
    pl.semaphore_signal(barrier, inc=1, device_id=partner, device_id_type=MESH)
    for o in XY:
        pl.semaphore_signal(barrier, inc=1, device_id=xy_peer(o), device_id_type=MESH)
    for d in Z_SEND:
        pl.semaphore_signal(barrier, inc=1, device_id=z_peer(d), device_id_type=MESH)

    for i in range(ZN):
        cols = slice(i * CHUNK, (i + 1) * CHUNK)
        rw[0, i] = rr_ref[:, cols]
        crv[i] = cr_ref[:, cols]
        lb[i] = jnp.broadcast_to(lab_ref[:, cols], (K_CHILD, CHUNK))

    def chunk_rows(zz):
        return pl.ds(pl.multiple_of(zz * CHUNK, CHUNK), CHUNK)

    def x_chunk(half, zz):
        return xv[half, chunk_rows(zz), :]

    for load in loads:
        load.wait()
    load_rc.wait()
    load_cc.wait()
    pl.semaphore_wait(barrier, 1 + len(XY) + len(Z_SEND))

    ag_w = None
    for it in range(ROOT_ITERS):
        mine = other = gram = None
        for d in [0] + Z_ARRIVAL:
            if it == 0:
                zz = z_at(d)
            else:
                zz = z_at(-d)
                if d:
                    ag_w[d].wait_recv()
            w = rw[it, zz]
            high, low = parts(w)
            other_d = nn(high, x_chunk(1, zz))
            mine_d = nn(high, x_chunk(0, zz))
            gram_d = gram3(high, low)
            other = other_d if other is None else other + other_d
            mine = mine_d if mine is None else mine + mine_d
            gram = gram_d if gram is None else gram + gram_d
        gram = padded(gram)
        rxs[it, :, 0:HALF] = other
        rxs[it, :, HALF:] = gram
        swap = send(rxs.at[it], rxr.at[it], s_rx.at[it], r_rx.at[it], partner)
        flush(1)
        swap.wait_recv()
        fr[it, p, :, 0:HALF] = mine + rxr[it, :, 0:HALF]
        fr[it, p, :, HALF:] = gram + rxr[it, :, HALF:]
        copies = [
            send(fr.at[it, p], fr.at[it, p], s_fr.at[it, i], r_fr.at[it, i], xy_peer(o))
            for i, o in enumerate(XY)
        ]
        flush(len(copies))
        for i in XY_ARRIVAL:
            copies[i].wait_recv()
        total = fr[it, 0]
        for q in range(1, CHIPS):
            total = total + fr[it, q]
        h = rh[it, 0]
        lower = small_product(total[:, HALF : HALF + K_ROOT], h, K_ROOT)
        h = h * total[:, 0:HALF] / lower
        rh[it + 1, 0] = h
        swap = send(rh.at[it + 1, 0], rh.at[it + 1, 1], s_rh.at[it], r_rh.at[it], partner)
        flush(1)
        high, low = parts(h)
        owns = {d: nt(high, x_chunk(0, z_at(d))) for d in Z_SEND + [0]}
        gram = gram3(high, low)
        swap.wait_recv()
        high, low = parts(rh[it + 1, 1])
        gram = padded(gram + gram3(high, low))
        copies = {}
        for d in Z_SEND + [0]:
            zs_r[it, d, :, 0:CHUNK] = owns[d] + nt(high, x_chunk(1, z_at(d)))
            zs_r[it, d, :, CHUNK:] = gram
            if d:
                copies[d] = send(zs_r.at[it, d], zr_r.at[it, d], s_zr.at[it, d], r_zr.at[it, d], z_peer(d))
        flush(len(copies))
        total = zs_r[it, 0]
        for d in Z_ARRIVAL:
            copies[d].wait_recv()
            total = total + zr_r[it, d]
        w = rw[it, z]
        lower = small_product(total[:, CHUNK : CHUNK + K_ROOT], w, K_ROOT)
        rw[it + 1, z] = w * total[:, 0:CHUNK] / lower
        ag_w = {
            d: send(rw.at[it + 1, z], rw.at[it + 1, z], s_rw.at[it, d], r_rw.at[it, d], z_peer(d))
            for d in Z_SEND
        }

    own16 = pl.ds(pl.multiple_of(child * K_CHILD, 16), K_CHILD)
    own8 = pl.ds(pl.multiple_of(p * 8, 8), 8)
    hb[0, 0, own16, :] = cc[...] * rh[ROOT_ITERS, 0, pl.ds(child, 1), :]

    def spread_of(zz, w):
        label = lb[zz]
        return jnp.concatenate([jnp.where(label == c, w, 0.0) for c in range(CHILDREN)], axis=0)

    lane_child = lax.div(lax.broadcasted_iota(jnp.int32, (K_CHILD, TOTAL), 1), K_CHILD)

    def diagonal(full):
        out = jnp.where(lane_child == 0, full[0:K_CHILD], 0.0)
        for c in range(1, CHILDREN):
            out = out + jnp.where(lane_child == c, full[c * K_CHILD : (c + 1) * K_CHILD], 0.0)
        return out

    for it in range(CHILD_ITERS):
        order = [0] + Z_ARRIVAL
        for d in order:
            zz = z_at(-d)
            if d:
                ag_w[d].wait_recv()
            if it == 0:
                label = lb[zz, 0:K_ROOT]
                ids = lax.broadcasted_iota(jnp.int32, (K_ROOT, CHUNK), 0)
                own_weight = jnp.sum(jnp.where(label == ids, rw[ROOT_ITERS, zz], 0.0), axis=0, keepdims=True)
                w = crv[zz] * own_weight
                cw[0, zz] = w
            else:
                w = cw[it, zz]
            high, low = parts(spread_of(zz, w))
            if d == 0:
                nps[it] = nn(high, x_chunk(1, zz))
                gacc[...] = gram3(high, low)
                no[...] = nn(high, x_chunk(0, zz))
            else:
                nps[it] += nn(high, x_chunk(1, zz))
                if d == order[-1]:
                    swap = send(nps.at[it], cxr.at[it], s_cx.at[it, 0], r_cx.at[it, 0], partner)
                gacc[...] += gram3(high, low)
                if d == order[-1]:
                    full = gacc[...]
                    gram = full[0:K_CHILD]
                    for c in range(1, CHILDREN):
                        gram = gram + full[c * K_CHILD : (c + 1) * K_CHILD]
                    gxs[it] = gram
                    swap_g = send(gxs.at[it], gxr.at[it], s_cx.at[it, 1], r_cx.at[it, 1], partner)
                no[...] += nn(high, x_chunk(0, zz))
        flush(2)
        swap_g.wait_recv()
        gram = gram + gxr[it]
        for c in range(CHILDREN):
            turned = gram if c == 0 else pltpu.roll(gram, TOTAL - c * K_CHILD, 1)
            rss[it, 2 * c, :, HALF:] = turned[0:8]
            rss[it, 2 * c + 1, :, HALF:] = turned[8:16]
        swap.wait_recv()
        for q in range(CHIPS):
            rss[it, q, :, 0:HALF] = no[8 * q : 8 * q + 8, :] + cxr[it, 8 * q : 8 * q + 8, :]
        copies = [
            send(rss.at[it, chip(*o)], rsr.at[it, i], s_rs.at[it, i], r_rs.at[it, i], xy_peer(o))
            for i, o in enumerate(XY)
        ]
        flush(len(copies))
        total = rss[it, p]
        for i in XY_ARRIVAL:
            copies[i].wait_recv()
            total = total + rsr[it, i]
        lower = small_product(total[:, HALF : HALF + K_CHILD], hb[it, 0, own16, :], K_CHILD)
        hb[it + 1, 0, own8, :] = hb[it, 0, own8, :] * total[:, 0:HALF] / lower
        own_h = hb.at[it + 1, 0, own8]
        copies = [
            send(own_h, own_h, s_ag.at[it, i], r_ag.at[it, i], xy_peer(o)) for i, o in enumerate(XY)
        ]
        relays = [send(own_h, hb.at[it + 1, 1, own8], s_re.at[it, 15], r_re.at[it, 15], partner)]
        flush(len(copies) + 1)
        for i in XY_ARRIVAL:
            copies[i].wait_recv()
            dx, dy = XY[i]
            rows = pl.ds(pl.multiple_of(chip(-dx, -dy) * 8, 8), 8)
            relays.append(
                send(hb.at[it + 1, 0, rows], hb.at[it + 1, 1, rows], s_re.at[it, i], r_re.at[it, i], partner)
            )
        high, low = parts(hb[it + 1, 0])
        hbb[0] = high
        for d in Z_SEND + [0]:
            acc[d] = nt(hbb[0], x_chunk(0, z_at(d)))
        full = gram3(high, low)
        flush(len(relays))
        for relay in relays:
            relay.wait_recv()
        high, low = parts(hb[it + 1, 1])
        hbb[1] = high
        gram = diagonal(full + gram3(high, low))
        copies = {}
        for d in Z_SEND + [0]:
            zz = z_at(d)
            label = lb[zz]
            rows_all = acc[d] + nt(hbb[1], x_chunk(1, zz))
            numer = jnp.where(label == 0, rows_all[0:K_CHILD], 0.0)
            for c in range(1, CHILDREN):
                numer = numer + jnp.where(label == c, rows_all[c * K_CHILD : (c + 1) * K_CHILD], 0.0)
            zs_c[it, d, :, 0:CHUNK] = numer
            zs_c[it, d, :, CHUNK:] = gram
            if d:
                copies[d] = send(zs_c.at[it, d], zr_c.at[it, d], s_zc.at[it, d], r_zc.at[it, d], z_peer(d))
        flush(len(copies))
        w = cw[it, z]
        s_high, s_low = parts(spread_of(z, w))
        total = zs_c[it, 0]
        for d in Z_ARRIVAL:
            copies[d].wait_recv()
            total = total + zr_c[it, d]
        g_high, g_low = parts(total[:, CHUNK:])
        lower = nn(g_high, s_high) + (nn(g_high, s_low) + nn(g_low, s_high))
        cw[it + 1, z] = w * total[:, 0:CHUNK] / lower
        ag_w = {
            d: send(cw.at[it + 1, z], cw.at[it + 1, z], s_cw.at[it, d], r_cw.at[it, d], z_peer(d))
            for d in Z_SEND
        }

    outs = [
        pltpu.make_async_copy(hb.at[CHILD_ITERS, 0], o_ch.at[:, own_cols], out_sem.at[0]),
        pltpu.make_async_copy(hb.at[CHILD_ITERS, 1], o_ch.at[:, other_cols], out_sem.at[1]),
        pltpu.make_async_copy(rh.at[ROOT_ITERS, 0], o_rh.at[:, own_cols], out_sem.at[2]),
        pltpu.make_async_copy(rh.at[ROOT_ITERS, 1], o_rh.at[:, other_cols], out_sem.at[3]),
    ]
    for out in outs:
        out.start()
    for i in range(ZN):
        o_rw[:, i * CHUNK : (i + 1) * CHUNK] = rw[ROOT_ITERS, i]
    flush(0)
    for d in Z_ARRIVAL:
        ag_w[d].wait_recv()
    for i in range(ZN):
        o_cw[:, i * CHUNK : (i + 1) * CHUNK] = cw[CHILD_ITERS, i]
    for out in outs:
        out.wait()


def body(matrix, labels, root_rows, root_cols, child_rows, child_cols):
    vmem = pl.BlockSpec(memory_space=pltpu.VMEM)
    hbm = pl.BlockSpec(memory_space=pl.ANY)
    dma = pltpu.SemaphoreType.DMA
    r, c = ROOT_ITERS, CHILD_ITERS
    n = len(XY)

    def v(*shape, dtype=F32):
        return pltpu.VMEM(shape, dtype)

    scratch = [
        v(2, NODES, HALF, dtype=BF16), v(K_CHILD, HALF), v(ZN, K_CHILD, CHUNK, dtype=jnp.int32),
        v(ZN, K_CHILD, CHUNK), v(r + 1, 2, K_ROOT, HALF), v(r + 1, ZN, K_ROOT, CHUNK),
        v(c + 1, ZN, K_CHILD, CHUNK), v(c + 1, 2, TOTAL, HALF), v(2, TOTAL, HALF, dtype=BF16),
        v(ZN, TOTAL, CHUNK), v(TOTAL, HALF), v(TOTAL, TOTAL),
        v(r, K_ROOT, HALF + 128), v(r, K_ROOT, HALF + 128), v(r, CHIPS, K_ROOT, HALF + 128),
        v(r, ZN, K_ROOT, CHUNK + 128), v(r, ZN, K_ROOT, CHUNK + 128),
        v(c, TOTAL, HALF), v(c, TOTAL, HALF), v(c, K_CHILD, TOTAL), v(c, K_CHILD, TOTAL),
        v(c, CHIPS, 8, HALF + 128), v(c, n, 8, HALF + 128),
        v(c, ZN, K_CHILD, CHUNK + 128), v(c, ZN, K_CHILD, CHUNK + 128),
        dma((10,)), dma((4,)),
        dma((r,)), dma((r,)), dma((r, n)), dma((r, n)), dma((r,)), dma((r,)),
        dma((r, ZN)), dma((r, ZN)), dma((r, ZN)), dma((r, ZN)),
        dma((c, 2)), dma((c, 2)), dma((c, n)), dma((c, n)), dma((c, n)), dma((c, n)),
        dma((c, n + 1)), dma((c, n + 1)), dma((c, ZN)), dma((c, ZN)), dma((c, ZN)), dma((c, ZN)),
    ]
    return pl.pallas_call(
        kernel,
        out_shape=(
            jax.ShapeDtypeStruct((K_ROOT, NODES), F32),
            jax.ShapeDtypeStruct((K_ROOT, BINS), F32),
            jax.ShapeDtypeStruct((K_CHILD, NODES), F32),
            jax.ShapeDtypeStruct((TOTAL, BINS), F32),
        ),
        in_specs=[hbm, vmem, vmem, hbm, vmem, hbm],
        out_specs=(vmem, hbm, vmem, hbm),
        scratch_shapes=scratch,
        compiler_params=pltpu.CompilerParams(
            collective_id=0, has_side_effects=True, vmem_limit_bytes=63 * 1024 * 1024
        ),
        name="nmf",
    )(matrix, labels.reshape(1, NODES), root_rows, root_cols, child_rows, child_cols)


def solution(mesh):
    return jax.shard_map(
        body,
        mesh=mesh,
        in_specs=(
            P("row", "col"), P("row", None), P(None, "row"),
            P(None, "col"), P(None, "row"), P(None, "col"),
        ),
        out_specs=(P(None, "row"), P(None, "col"), P(None, "row"), P(None, "col")),
        check_vma=False,
    )
```

```python
import jax
import jax.numpy as jnp
from jax import lax
from jax.experimental import pallas as pl
from jax.experimental.pallas import tpu as pltpu
from jax.sharding import PartitionSpec as P

MESH = pl.DeviceIdType.MESH
F32, BF16 = jnp.float32, jnp.bfloat16
K_ROOT, K_CHILD, CHILDREN = 8, 16, 8
ROOT_ITERS, CHILD_ITERS = 2, 3
TOTAL = CHILDREN * K_CHILD
NODES, BINS, HALF = 2048, 1024, 512
ZN, CHUNK = 8, 256
CHIPS = 16


def ring(d, n):
    return min(d, n - d)


XY = sorted(
    [(dx, dy) for dx in range(4) for dy in range(4) if dx or dy],
    key=lambda o: -(ring(o[0], 4) + ring(o[1], 4)),
)
XY_ARRIVAL = list(reversed(range(len(XY))))
Z_SEND = [(e, d) for d in (4, 3, 5, 2, 6, 1, 7) for e in (0, 1)] + [(1, 0)]
Z_ARRIVAL = [(1, 0)] + [(e, d) for d in (1, 7, 2, 6, 3, 5, 4) for e in (0, 1)]
GROUPS = [[(0, 0)], [(1, 0)]] + [[(0, d), (1, d)] for d in (1, 7, 2, 6, 3, 5, 4)]


def nn(a, b):
    return jnp.dot(a, b, preferred_element_type=F32)


def nt(a, b):
    return lax.dot_general(a, b, (((1,), (1,)), ((), ())), preferred_element_type=F32)


def parts(a):
    high = a.astype(BF16)
    return high, (a - high.astype(F32)).astype(BF16)


def gram3(high, low):
    return nt(high, high) + (nt(high, low) + nt(low, high))


def padded(gram):
    rows, cols = gram.shape
    return jnp.concatenate([gram, jnp.zeros((rows, 128 - cols), F32)], axis=1)


def small_product(gram, rows, count):
    total = gram[:, 0:1] * rows[0:1, :]
    for k in range(1, count):
        total = total + gram[:, k : k + 1] * rows[k : k + 1, :]
    return total


def plus(a, b):
    return b if a is None else a + b


def kernel(
    x_hbm, lab_ref, rr_ref, rc_hbm, cr_ref, cc_hbm,
    o_rw, o_rh, o_cw, o_ch,
    xv, xo, xs, xr, cc, lab_other, cr_other, lb, crv,
    rh, rh_other, rw, cw, hb, hb_other, hbb, no, gacc,
    rxs, rxr, fr, zs_r, zr_r, rss, rsr, zs_c, zr_c,
    in_sem, s_x, r_x, s_m, r_m,
    s_fr, r_fr, s_zr, r_zr, s_rw, r_rw, s_rs, r_rs, s_ag, r_ag, s_zc, r_zc, s_cw, r_cw,
):
    row, z = lax.axis_index("row"), lax.axis_index("col")
    p, core = lax.div(row, 2), lax.rem(row, 2)
    x, y = lax.div(p, 4), lax.rem(p, 4)
    child = lax.div(p, 2)

    def chip(dx, dy):
        return lax.rem(x + dx + 4, 4) * 4 + lax.rem(y + dy + 4, 4)

    def xy_peer(o):
        return {"row": chip(*o) * 2 + core, "col": z}

    def z_at(d):
        return lax.rem(z + d + ZN, ZN)

    def z_peer(ed):
        e, d = ed
        return {"row": p * 2 + (core if e == 0 else 1 - core), "col": z_at(d)}

    partner = z_peer((1, 0))
    pending = []

    def send(src, dst, ssem, rsem, device):
        copy = pltpu.make_async_remote_copy(
            src_ref=src, dst_ref=dst, send_sem=ssem, recv_sem=rsem,
            device_id=device, device_id_type=MESH,
        )
        copy.start()
        pending.append(copy)
        return copy

    def flush(keep):
        while len(pending) > keep:
            pending.pop(0).wait_send()

    own_cols = pl.ds(pl.multiple_of(HALF * core, HALF), HALF)
    other_cols = pl.ds(pl.multiple_of(HALF * (1 - core), HALF), HALF)
    loads = []
    for i in range(4):
        rows = pl.ds(i * 512, 512)
        loads.append(pltpu.make_async_copy(x_hbm.at[rows, other_cols], xo.at[rows], in_sem.at[2 * i]))
        loads.append(pltpu.make_async_copy(x_hbm.at[rows, own_cols], xv.at[0, rows], in_sem.at[2 * i + 1]))
    load_cc = pltpu.make_async_copy(
        cc_hbm.at[pl.ds(pl.multiple_of(child * K_CHILD, 16), K_CHILD), own_cols], cc, in_sem.at[8]
    )
    load_rc = pltpu.make_async_copy(rc_hbm.at[:, own_cols], rh.at[0], in_sem.at[9])
    for load in loads:
        load.start()
    load_rc.start()
    load_cc.start()

    barrier = pltpu.get_barrier_semaphore()
    for o in XY:
        pl.semaphore_signal(barrier, inc=1, device_id=xy_peer(o), device_id_type=MESH)
    for ed in Z_SEND:
        pl.semaphore_signal(barrier, inc=1, device_id=z_peer(ed), device_id_type=MESH)

    def cols_of(i):
        return slice(i * CHUNK, (i + 1) * CHUNK)

    for i in range(ZN):
        rw[0, 0, i] = rr_ref[:, cols_of(i)]
        crv[0, i] = cr_ref[:, cols_of(i)]
        lb[0, i] = jnp.broadcast_to(lab_ref[:, cols_of(i)], (K_CHILD, CHUNK))

    def x_chunk(e, zz):
        return xv[e, pl.ds(pl.multiple_of(zz * CHUNK, CHUNK), CHUNK), :]

    ag_w = None
    for it in range(ROOT_ITERS):
        mine = gram = None
        if it == 0:
            other = None
            for i in range(ZN):
                if i % 2 == 0:
                    loads[i].wait()
                    loads[i + 1].wait()
                rows = pl.ds(i * CHUNK, CHUNK)
                high, low = parts(rw[0, 0, i])
                other = plus(other, nn(high, xo[rows, :]))
                mine = plus(mine, nn(high, xv[0, rows, :]))
                gram = plus(gram, gram3(high, low))
            load_rc.wait()
            load_cc.wait()
            gram = padded(gram)
            rxs[:, 0:HALF] = other
            rxs[:, HALF:] = gram
            pl.semaphore_wait(barrier, len(XY) + len(Z_SEND))
            swap = send(rxs, rxr, s_m.at[0], r_m.at[0], partner)
            x_copies = []

            def pass_on(i):
                rows = pl.ds(i * CHUNK, CHUNK)
                xs[rows, :] = xo[rows, :].astype(F32)
                x_copies.append(send(xs.at[rows], xr.at[rows], s_x.at[i], r_x.at[i], partner))

            for i in range(3):
                pass_on(i)
            swap.wait_recv()
            mine = mine + rxr[:, 0:HALF]
            gram = gram + rxr[:, HALF:]
        else:
            for group in GROUPS:
                for e, d in group:
                    if (e, d) != (0, 0):
                        ag_w[e, d].wait_recv()
                    zz = z_at(-d)
                    high, low = parts(rw[it, e, zz])
                    mine = plus(mine, nn(high, x_chunk(e, zz)))
                    gram = plus(gram, gram3(high, low))
            gram = padded(gram)
        fr[it, p, :, 0:HALF] = mine
        fr[it, p, :, HALF:] = gram
        copies = [
            send(fr.at[it, p], fr.at[it, p], s_fr.at[it, i], r_fr.at[it, i], xy_peer(o))
            for i, o in enumerate(XY)
        ]
        if it == 0:
            for i in range(3, ZN):
                pass_on(i)
            small = [
                send(lab_ref, lab_other, s_m.at[1], r_m.at[1], partner),
                send(cr_ref, cr_other, s_m.at[2], r_m.at[2], partner),
            ]
            for i in range(ZN):
                x_copies[i].wait_recv()
                rows = pl.ds(i * CHUNK, CHUNK)
                xv[1, rows, :] = xr[rows, :].astype(BF16)
            for copy in small:
                copy.wait_recv()
            for i in range(ZN):
                crv[1, i] = cr_other[:, cols_of(i)]
                lb[1, i] = jnp.broadcast_to(lab_other[:, cols_of(i)], (K_CHILD, CHUNK))
        else:
            flush(len(copies))
        for i in XY_ARRIVAL:
            copies[i].wait_recv()
        total = fr[it, 0]
        for q in range(1, CHIPS):
            total = total + fr[it, q]
        h = rh[it]
        lower = small_product(total[:, HALF : HALF + K_ROOT], h, K_ROOT)
        h = h * total[:, 0:HALF] / lower
        rh[it + 1] = h
        high, low = parts(h)
        gram = padded(gram3(high, low))
        copies = {}
        for e, d in Z_SEND + [(0, 0)]:
            zs_r[it, e, d, :, 0:CHUNK] = nt(high, x_chunk(e, z_at(d)))
            zs_r[it, e, d, :, CHUNK:] = gram
            if (e, d) != (0, 0):
                copies[e, d] = send(
                    zs_r.at[it, e, d], zr_r.at[it, e, d], s_zr.at[it, e, d], r_zr.at[it, e, d], z_peer((e, d))
                )
        flush(len(copies))
        total = zs_r[it, 0, 0]
        for e, d in Z_ARRIVAL:
            copies[e, d].wait_recv()
            total = total + zr_r[it, e, d]
        w = rw[it, 0, z]
        lower = small_product(total[:, CHUNK : CHUNK + K_ROOT], w, K_ROOT)
        rw[it + 1, 0, z] = w * total[:, 0:CHUNK] / lower
        ag_w = {
            (e, d): send(
                rw.at[it + 1, 0, z], rw.at[it + 1, e, z], s_rw.at[it, e, d], r_rw.at[it, e, d], z_peer((e, d))
            )
            for e, d in Z_SEND
        }
    rh_swap = send(rh.at[ROOT_ITERS], rh_other, s_m.at[3], r_m.at[3], partner)

    own16 = pl.ds(pl.multiple_of(child * K_CHILD, 16), K_CHILD)
    own8 = pl.ds(pl.multiple_of(p * 8, 8), 8)
    hb[0, own16, :] = cc[...] * rh[ROOT_ITERS, pl.ds(child, 1), :]

    def spread_of(e, zz, w):
        label = lb[e, zz]
        return jnp.concatenate([jnp.where(label == c, w, 0.0) for c in range(CHILDREN)], axis=0)

    lane_child = lax.div(lax.broadcasted_iota(jnp.int32, (K_CHILD, TOTAL), 1), K_CHILD)

    def diagonal(full):
        out = None
        for c in range(CHILDREN):
            out = plus(out, jnp.where(lane_child == c, full[c * K_CHILD : (c + 1) * K_CHILD], 0.0))
        return out

    for it in range(CHILD_ITERS):
        for g, group in enumerate(GROUPS):
            numer = gram = None
            for e, d in group:
                zz = z_at(-d)
                if (e, d) != (0, 0):
                    ag_w[e, d].wait_recv()
                if it == 0:
                    label = lb[e, zz, 0:K_ROOT]
                    ids = lax.broadcasted_iota(jnp.int32, (K_ROOT, CHUNK), 0)
                    own_weight = jnp.sum(
                        jnp.where(label == ids, rw[ROOT_ITERS, e, zz], 0.0), axis=0, keepdims=True
                    )
                    w = crv[e, zz] * own_weight
                    cw[0, e, zz] = w
                else:
                    w = cw[it, e, zz]
                high, low = parts(spread_of(e, zz, w))
                numer = plus(numer, nn(high, x_chunk(e, zz)))
                both = jnp.concatenate([high, low], axis=0)
                gram = plus(gram, nt(both, jnp.concatenate(parts(w), axis=0)))
            if g == 0:
                no[...] = numer
                gacc[...] = gram
            elif g < len(GROUPS) - 1:
                no[...] += numer
                gacc[...] += gram
        numer = no[...] + numer
        gram = gacc[...] + gram
        gram = padded(
            gram[0:TOTAL, 0:K_CHILD] + (gram[0:TOTAL, K_CHILD:] + gram[TOTAL:, 0:K_CHILD])
        )
        for q in range(CHIPS):
            rss[it, q, :, 0:HALF] = numer[8 * q : 8 * q + 8]
            rss[it, q, :, HALF:] = gram[8 * q : 8 * q + 8]
        copies = [
            send(rss.at[it, chip(*o)], rsr.at[it, i], s_rs.at[it, i], r_rs.at[it, i], xy_peer(o))
            for i, o in enumerate(XY)
        ]
        flush(len(copies))
        total = rss[it, p]
        for i in XY_ARRIVAL:
            copies[i].wait_recv()
            total = total + rsr[it, i]
        lower = small_product(total[:, HALF : HALF + K_CHILD], hb[it, own16, :], K_CHILD)
        hb[it + 1, own8, :] = hb[it, own8, :] * total[:, 0:HALF] / lower
        own_h = hb.at[it + 1, own8]
        copies = [
            send(own_h, own_h, s_ag.at[it, i], r_ag.at[it, i], xy_peer(o)) for i, o in enumerate(XY)
        ]
        flush(len(copies))
        for i in XY_ARRIVAL:
            copies[i].wait_recv()
        if it == CHILD_ITERS - 1:
            hb_swap = send(hb.at[it + 1], hb_other, s_m.at[4], r_m.at[4], partner)
        high, low = parts(hb[it + 1])
        hbb[...] = high
        full = nt(jnp.concatenate([high, low], axis=0), high)
        gram = diagonal(full[0:TOTAL] + (full[TOTAL:] + full[TOTAL:].T))
        copies = {}
        for e, d in Z_SEND + [(0, 0)]:
            zz = z_at(d)
            label = lb[e, zz]
            rows_all = nt(hbb[...], x_chunk(e, zz))
            numer = None
            for c in range(CHILDREN):
                numer = plus(numer, jnp.where(label == c, rows_all[c * K_CHILD : (c + 1) * K_CHILD], 0.0))
            zs_c[it, e, d, :, 0:CHUNK] = numer
            zs_c[it, e, d, :, CHUNK:] = gram
            if (e, d) != (0, 0):
                copies[e, d] = send(
                    zs_c.at[it, e, d], zr_c.at[it, e, d], s_zc.at[it, e, d], r_zc.at[it, e, d], z_peer((e, d))
                )
        flush(len(copies))
        w = cw[it, 0, z]
        s_high, s_low = parts(spread_of(0, z, w))
        total = zs_c[it, 0, 0]
        for e, d in Z_ARRIVAL:
            copies[e, d].wait_recv()
            total = total + zr_c[it, e, d]
        g_high, g_low = parts(total[:, CHUNK:])
        lower = nn(g_high, s_high) + (nn(g_high, s_low) + nn(g_low, s_high))
        cw[it + 1, 0, z] = w * total[:, 0:CHUNK] / lower
        last = it == CHILD_ITERS - 1
        ag_w = {
            (e, d): send(
                cw.at[it + 1, 0, z], cw.at[it + 1, e, z], s_cw.at[it, e, d], r_cw.at[it, e, d], z_peer((e, d))
            )
            for e, d in Z_SEND
            if e == 0 or not last
        }

    rh_swap.wait_recv()
    o_rh[:, own_cols] = rh[ROOT_ITERS]
    o_rh[:, other_cols] = rh_other[...]
    hb_swap.wait_recv()
    o_ch[:, own_cols] = hb[CHILD_ITERS]
    o_ch[:, other_cols] = hb_other[...]
    for i in range(ZN):
        o_rw[:, cols_of(i)] = rw[ROOT_ITERS, 0, i]
    flush(0)
    for e, d in Z_ARRIVAL:
        if (e, d) in ag_w:
            ag_w[e, d].wait_recv()
    for i in range(ZN):
        o_cw[:, cols_of(i)] = cw[CHILD_ITERS, 0, i]


def put_out(*refs):
    sources, targets, sem = refs[:4], refs[4:8], refs[8]
    copies = [pltpu.make_async_copy(s, t, sem.at[i]) for i, (s, t) in enumerate(zip(sources, targets))]
    for copy in copies:
        copy.start()
    for copy in copies:
        copy.wait()


def body(matrix, labels, root_rows, root_cols, child_rows, child_cols):
    vmem = pl.BlockSpec(memory_space=pltpu.VMEM)
    hbm = pl.BlockSpec(memory_space=pltpu.HBM)
    dma = pltpu.SemaphoreType.DMA
    r, c = ROOT_ITERS, CHILD_ITERS
    n = len(XY)

    def v(*shape, dtype=F32):
        return pltpu.VMEM(shape, dtype)

    i32 = jnp.int32
    scratch = [
        v(2, NODES, HALF, dtype=BF16), v(NODES, HALF, dtype=BF16), v(NODES, HALF), v(NODES, HALF),
        v(K_CHILD, HALF), v(1, NODES, dtype=i32), v(K_CHILD, NODES),
        v(2, ZN, K_CHILD, CHUNK, dtype=i32), v(2, ZN, K_CHILD, CHUNK),
        v(r + 1, K_ROOT, HALF), v(K_ROOT, HALF), v(r + 1, 2, ZN, K_ROOT, CHUNK),
        v(c + 1, 2, ZN, K_CHILD, CHUNK), v(c + 1, TOTAL, HALF), v(TOTAL, HALF),
        v(TOTAL, HALF, dtype=BF16), v(TOTAL, HALF), v(2 * TOTAL, 2 * K_CHILD),
        v(K_ROOT, HALF + 128), v(K_ROOT, HALF + 128), v(r, CHIPS, K_ROOT, HALF + 128),
        v(r, 2, ZN, K_ROOT, CHUNK + 128), v(r, 2, ZN, K_ROOT, CHUNK + 128),
        v(c, CHIPS, 8, HALF + 128), v(c, n, 8, HALF + 128),
        v(c, 2, ZN, K_CHILD, CHUNK + 128), v(c, 2, ZN, K_CHILD, CHUNK + 128),
        dma((10,)), dma((ZN,)), dma((ZN,)), dma((5,)), dma((5,)),
        dma((r, n)), dma((r, n)), dma((r, 2, ZN)), dma((r, 2, ZN)), dma((r, 2, ZN)), dma((r, 2, ZN)),
        dma((c, n)), dma((c, n)), dma((c, n)), dma((c, n)),
        dma((c, 2, ZN)), dma((c, 2, ZN)), dma((c, 2, ZN)), dma((c, 2, ZN)),
    ]
    shapes = (
        jax.ShapeDtypeStruct((K_ROOT, NODES), F32),
        jax.ShapeDtypeStruct((K_ROOT, BINS), F32),
        jax.ShapeDtypeStruct((K_CHILD, NODES), F32),
        jax.ShapeDtypeStruct((TOTAL, BINS), F32),
    )
    outs = pl.pallas_call(
        kernel,
        out_shape=shapes,
        in_specs=[hbm, vmem, vmem, hbm, vmem, hbm],
        out_specs=(vmem,) * 4,
        scratch_shapes=scratch,
        compiler_params=pltpu.CompilerParams(
            collective_id=0, has_side_effects=True, vmem_limit_bytes=54000000
        ),
        name="nmf",
    )(matrix, labels.reshape(1, NODES), root_rows, root_cols, child_rows, child_cols)
    return pl.pallas_call(
        put_out,
        out_shape=shapes,
        in_specs=[vmem] * 4,
        out_specs=(hbm,) * 4,
        scratch_shapes=[dma((4,))],
        compiler_params=pltpu.CompilerParams(vmem_limit_bytes=4 * 1024 * 1024),
        name="put_out",
    )(*outs)


def solution(mesh):
    return jax.shard_map(
        body,
        mesh=mesh,
        in_specs=(
            P("row", "col"), P("row", None), P(None, "row"),
            P(None, "col"), P(None, "row"), P(None, "col"),
        ),
        out_specs=(P(None, "row"), P(None, "col"), P(None, "row"), P(None, "col")),
        check_vma=False,
    )
```

```python
import jax
import jax.numpy as jnp
from jax import lax
from jax.experimental import pallas as pl
from jax.experimental.pallas import tpu as pltpu
from jax.sharding import PartitionSpec as P

MESH = pl.DeviceIdType.MESH
F32, BF16 = jnp.float32, jnp.bfloat16
K_ROOT, K_CHILD, CHILDREN = 8, 16, 8
ROOT_ITERS, CHILD_ITERS = 2, 3
TOTAL = CHILDREN * K_CHILD
NODES, BINS, HALF = 2048, 1024, 512
ZN, CHUNK = 8, 256
CHIPS = 16


def ring(d, n):
    return min(d, n - d)


XY = sorted(
    [(dx, dy) for dx in range(4) for dy in range(4) if dx or dy],
    key=lambda o: -(ring(o[0], 4) + ring(o[1], 4)),
)
XY_ARRIVAL = list(reversed(range(len(XY))))
Z_SEND = [4, 3, 5, 2, 6, 1, 7]
Z_ARRIVAL = [1, 7, 2, 6, 3, 5, 4]
GROUPS = [[(0, 0)]] + [[(0, d), (1, p)] for d, p in zip(Z_ARRIVAL, [0] + Z_ARRIVAL)] + [[(1, 4)]]


def nn(a, b):
    return jnp.dot(a, b, preferred_element_type=F32)


def nt(a, b):
    return lax.dot_general(a, b, (((1,), (1,)), ((), ())), preferred_element_type=F32)


def parts(a):
    high = a.astype(BF16)
    return high, (a - high.astype(F32)).astype(BF16)


def gram3(high, low):
    return nt(high, high) + (nt(high, low) + nt(low, high))


def padded(gram):
    rows, cols = gram.shape
    return jnp.concatenate([gram, jnp.zeros((rows, 128 - cols), F32)], axis=1)


def small_product(gram, rows, count):
    total = gram[:, 0:1] * rows[0:1, :]
    for k in range(1, count):
        total = total + gram[:, k : k + 1] * rows[k : k + 1, :]
    return total


def plus(a, b):
    return b if a is None else a + b


def kernel(
    x_hbm, lab_ref, rr_ref, rc_hbm, cr_ref, cc_hbm,
    o_rw, o_rh, o_cw, o_ch,
    xv, xo, xs, xr, cc, lab_other, cr_other, lb, crv,
    rh, rh_other, rw, cw, hb, hb_other, hbb, no, gacc,
    rxs, rxr, fr, zs_r, zr_r, rss, rsr, zs_c, zr_c, gxs, gxr,
    in_sem, s_x, r_x, s_m, r_m,
    s_fr, r_fr, s_zr, r_zr, s_rw, r_rw, s_rs, r_rs, s_ag, r_ag, s_zc, r_zc, s_cw, r_cw, s_g, r_g, out_sem,
):
    row, z = lax.axis_index("row"), lax.axis_index("col")
    p, core = lax.div(row, 2), lax.rem(row, 2)
    x, y = lax.div(p, 4), lax.rem(p, 4)
    child = lax.div(p, 2)

    def chip(dx, dy):
        return lax.rem(x + dx + 4, 4) * 4 + lax.rem(y + dy + 4, 4)

    def xy_peer(o):
        return {"row": chip(*o) * 2 + core, "col": z}

    def z_at(d):
        return lax.rem(z + d + ZN, ZN)

    def z_peer(d):
        return {"row": row, "col": z_at(d)}

    partner = {"row": p * 2 + 1 - core, "col": z}
    pending = []

    def send(src, dst, ssem, rsem, device):
        copy = pltpu.make_async_remote_copy(
            src_ref=src, dst_ref=dst, send_sem=ssem, recv_sem=rsem,
            device_id=device, device_id_type=MESH,
        )
        copy.start()
        pending.append(copy)
        return copy

    def flush(keep):
        while len(pending) > keep:
            pending.pop(0).wait_send()

    own_cols = pl.ds(pl.multiple_of(HALF * core, HALF), HALF)
    other_cols = pl.ds(pl.multiple_of(HALF * (1 - core), HALF), HALF)
    loads = []
    for i in range(4):
        rows = pl.ds(i * 512, 512)
        loads.append(pltpu.make_async_copy(x_hbm.at[rows, other_cols], xo.at[rows], in_sem.at[2 * i]))
        loads.append(pltpu.make_async_copy(x_hbm.at[rows, own_cols], xv.at[0, rows], in_sem.at[2 * i + 1]))
    load_cc = pltpu.make_async_copy(
        cc_hbm.at[pl.ds(pl.multiple_of(child * K_CHILD, 16), K_CHILD), own_cols], cc, in_sem.at[8]
    )
    load_rc = pltpu.make_async_copy(rc_hbm.at[:, own_cols], rh.at[0], in_sem.at[9])
    for load in loads:
        load.start()
    load_rc.start()
    load_cc.start()

    barrier = pltpu.get_barrier_semaphore()
    for o in XY:
        pl.semaphore_signal(barrier, inc=1, device_id=xy_peer(o), device_id_type=MESH)
    for d in Z_SEND:
        pl.semaphore_signal(barrier, inc=1, device_id=z_peer(d), device_id_type=MESH)
    pl.semaphore_signal(barrier, inc=1, device_id=partner, device_id_type=MESH)

    def cols_of(i):
        return slice(i * CHUNK, (i + 1) * CHUNK)

    for i in range(ZN):
        rw[0, 0, i] = rr_ref[:, cols_of(i)]
        crv[0, i] = cr_ref[:, cols_of(i)]
        lb[0, i] = jnp.broadcast_to(lab_ref[:, cols_of(i)], (K_CHILD, CHUNK))

    def x_chunk(e, zz):
        return xv[e, pl.ds(pl.multiple_of(zz * CHUNK, CHUNK), CHUNK), :]

    class Spread:
        def __init__(self, ref, ssem, rsem):
            self.ref, self.ssem, self.rsem = ref, ssem, rsem
            own = ref.at[0, z]
            self.along = {d: send(own, own, ssem.at[0, d], rsem.at[0, d], z_peer(d)) for d in Z_SEND}
            self.across = {}
            self.relay(0)

        def relay(self, d):
            zz = z_at(-d)
            self.across[d] = send(
                self.ref.at[0, zz], self.ref.at[1, zz], self.ssem.at[1, d], self.rsem.at[1, d], partner
            )

        def arrive(self, e, d):
            if e == 1:
                self.across[d].wait_recv()
            elif d:
                self.along[d].wait_recv()
                self.relay(d)

    ag_w = None
    for it in range(ROOT_ITERS):
        mine = gram = None
        if it == 0:
            other = None
            for i in range(ZN):
                if i % 2 == 0:
                    loads[i].wait()
                    loads[i + 1].wait()
                rows = pl.ds(i * CHUNK, CHUNK)
                high, low = parts(rw[0, 0, i])
                other = plus(other, nn(high, xo[rows, :]))
                mine = plus(mine, nn(high, xv[0, rows, :]))
                gram = plus(gram, gram3(high, low))
            load_rc.wait()
            load_cc.wait()
            gram = padded(gram)
            rxs[:, 0:HALF] = other
            rxs[:, HALF:] = gram
            pl.semaphore_wait(barrier, len(XY) + len(Z_SEND) + 1)
            swap = send(rxs, rxr, s_m.at[0], r_m.at[0], partner)
            x_copies = []

            def pass_on(i):
                rows = pl.ds(i * CHUNK, CHUNK)
                xs[rows, :] = xo[rows, :].astype(F32)
                x_copies.append(send(xs.at[rows], xr.at[rows], s_x.at[i], r_x.at[i], partner))

            for i in range(3):
                pass_on(i)
            swap.wait_recv()
            mine = mine + rxr[:, 0:HALF]
            gram = gram + rxr[:, HALF:]
        else:
            for group in GROUPS:
                for e, d in group:
                    ag_w.arrive(e, d)
                    zz = z_at(-d)
                    high, low = parts(rw[it, e, zz])
                    mine = plus(mine, nn(high, x_chunk(e, zz)))
                    gram = plus(gram, gram3(high, low))
            gram = padded(gram)
        fr[it, p, :, 0:HALF] = mine
        fr[it, p, :, HALF:] = gram
        copies = [
            send(fr.at[it, p], fr.at[it, p], s_fr.at[it, i], r_fr.at[it, i], xy_peer(o))
            for i, o in enumerate(XY)
        ]
        if it == 0:
            for i in range(3, ZN):
                pass_on(i)
            small = [
                send(lab_ref, lab_other, s_m.at[1], r_m.at[1], partner),
                send(cr_ref, cr_other, s_m.at[2], r_m.at[2], partner),
            ]
            for i in range(ZN):
                x_copies[i].wait_recv()
                rows = pl.ds(i * CHUNK, CHUNK)
                xv[1, rows, :] = xr[rows, :].astype(BF16)
            for copy in small:
                copy.wait_recv()
            for i in range(ZN):
                crv[1, i] = cr_other[:, cols_of(i)]
                lb[1, i] = jnp.broadcast_to(lab_other[:, cols_of(i)], (K_CHILD, CHUNK))
        else:
            flush(len(copies))
        for i in XY_ARRIVAL:
            copies[i].wait_recv()
        total = fr[it, 0]
        for q in range(1, CHIPS):
            total = total + fr[it, q]
        h = rh[it]
        lower = small_product(total[:, HALF : HALF + K_ROOT], h, K_ROOT)
        h = h * total[:, 0:HALF] / lower
        rh[it + 1] = h
        high, low = parts(h)
        gram = padded(gram3(high, low))
        across, copies = {}, {}
        for d in Z_SEND + [0]:
            zs_r[it, 1, d, :, 0:CHUNK] = nt(high, x_chunk(1, z_at(d)))
            zs_r[it, 1, d, :, CHUNK:] = gram
            across[d] = send(zs_r.at[it, 1, d], zr_r.at[it, 1, d], s_zr.at[it, 1, d], r_zr.at[it, 1, d], partner)
        owns = [nt(high, x_chunk(0, z_at(d))) for d in Z_SEND + [0]]
        for own, d in zip(owns, Z_SEND + [0]):
            across[d].wait_recv()
            zs_r[it, 0, d, :, 0:CHUNK] = own + zr_r[it, 1, d, :, 0:CHUNK]
            zs_r[it, 0, d, :, CHUNK:] = gram + zr_r[it, 1, d, :, CHUNK:]
            if d:
                copies[d] = send(
                    zs_r.at[it, 0, d], zr_r.at[it, 0, d], s_zr.at[it, 0, d], r_zr.at[it, 0, d], z_peer(d)
                )
        flush(len(copies))
        total = zs_r[it, 0, 0]
        for d in Z_ARRIVAL:
            copies[d].wait_recv()
            total = total + zr_r[it, 0, d]
        w = rw[it, 0, z]
        lower = small_product(total[:, CHUNK : CHUNK + K_ROOT], w, K_ROOT)
        rw[it + 1, 0, z] = w * total[:, 0:CHUNK] / lower
        ag_w = Spread(rw.at[it + 1], s_rw.at[it], r_rw.at[it])
    rh_swap = send(rh.at[ROOT_ITERS], rh_other, s_m.at[3], r_m.at[3], partner)

    own16 = pl.ds(pl.multiple_of(child * K_CHILD, 16), K_CHILD)
    own8 = pl.ds(pl.multiple_of(p * 8, 8), 8)
    hb[0, own16, :] = cc[...] * rh[ROOT_ITERS, pl.ds(child, 1), :]

    def spread_of(e, zz, w):
        label = lb[e, zz]
        return jnp.concatenate([jnp.where(label == c, w, 0.0) for c in range(CHILDREN)], axis=0)

    lane_child = lax.div(lax.broadcasted_iota(jnp.int32, (K_CHILD, TOTAL), 1), K_CHILD)

    def diagonal(full):
        out = None
        for c in range(CHILDREN):
            out = plus(out, jnp.where(lane_child == c, full[c * K_CHILD : (c + 1) * K_CHILD], 0.0))
        return out

    for it in range(CHILD_ITERS):
        for g, group in enumerate(GROUPS):
            numer = gram = None
            for e, d in group:
                zz = z_at(-d)
                ag_w.arrive(e, d)
                if it == 0:
                    label = lb[e, zz, 0:K_ROOT]
                    ids = lax.broadcasted_iota(jnp.int32, (K_ROOT, CHUNK), 0)
                    own_weight = jnp.sum(
                        jnp.where(label == ids, rw[ROOT_ITERS, e, zz], 0.0), axis=0, keepdims=True
                    )
                    w = crv[e, zz] * own_weight
                    cw[0, e, zz] = w
                else:
                    w = cw[it, e, zz]
                high, low = parts(spread_of(e, zz, w))
                numer = plus(numer, nn(high, x_chunk(e, zz)))
                both = jnp.concatenate([high, low], axis=0)
                gram = plus(gram, nt(both, jnp.concatenate(parts(w), axis=0)))
            if g == 0:
                no[...] = numer
                gacc[...] = gram
            elif g < len(GROUPS) - 1:
                no[...] += numer
                gacc[...] += gram
        numer = no[...] + numer
        gram = gacc[...] + gram
        gram = padded(
            gram[0:TOTAL, 0:K_CHILD] + (gram[0:TOTAL, K_CHILD:] + gram[TOTAL:, 0:K_CHILD])
        )
        for q in range(CHIPS):
            rss[it, q, :, 0:HALF] = numer[8 * q : 8 * q + 8]
            rss[it, q, :, HALF:] = gram[8 * q : 8 * q + 8]
        copies = [
            send(rss.at[it, chip(*o)], rsr.at[it, i], s_rs.at[it, i], r_rs.at[it, i], xy_peer(o))
            for i, o in enumerate(XY)
        ]
        flush(len(copies))
        total = rss[it, p]
        for i in XY_ARRIVAL:
            copies[i].wait_recv()
            total = total + rsr[it, i]
        lower = small_product(total[:, HALF : HALF + K_CHILD], hb[it, own16, :], K_CHILD)
        hb[it + 1, own8, :] = hb[it, own8, :] * total[:, 0:HALF] / lower
        own_h = hb.at[it + 1, own8]
        copies = [
            send(own_h, own_h, s_ag.at[it, i], r_ag.at[it, i], xy_peer(o)) for i, o in enumerate(XY)
        ]
        flush(len(copies))
        for i in XY_ARRIVAL:
            copies[i].wait_recv()
        if it == CHILD_ITERS - 1:
            hb_swap = send(hb.at[it + 1], hb_other, s_m.at[4], r_m.at[4], partner)
        high, low = parts(hb[it + 1])
        hbb[...] = high
        full = nt(jnp.concatenate([high, low], axis=0), high)
        gram = diagonal(full[0:TOTAL] + (full[TOTAL:] + full[TOTAL:].T))
        def numer_of(e, zz):
            label = lb[e, zz]
            rows_all = nt(hbb[...], x_chunk(e, zz))
            numer = None
            for c in range(CHILDREN):
                numer = plus(numer, jnp.where(label == c, rows_all[c * K_CHILD : (c + 1) * K_CHILD], 0.0))
            return numer

        gxs[it] = gram
        swap_g = send(gxs.at[it], gxr.at[it], s_g.at[it], r_g.at[it], partner)
        across, copies = {}, {}
        for d in Z_SEND + [0]:
            zs_c[it, 1, d, :, 0:CHUNK] = numer_of(1, z_at(d))
            across[d] = send(
                zs_c.at[it, 1, d, :, 0:CHUNK], zr_c.at[it, 1, d, :, 0:CHUNK],
                s_zc.at[it, 1, d], r_zc.at[it, 1, d], partner,
            )
        for d in Z_SEND + [0]:
            numer = numer_of(0, z_at(d))
            if d == Z_SEND[0]:
                swap_g.wait_recv()
                gram = gram + gxr[it]
            across[d].wait_recv()
            zs_c[it, 0, d, :, 0:CHUNK] = numer + zr_c[it, 1, d, :, 0:CHUNK]
            zs_c[it, 0, d, :, CHUNK:] = gram
            if d:
                copies[d] = send(
                    zs_c.at[it, 0, d], zr_c.at[it, 0, d], s_zc.at[it, 0, d], r_zc.at[it, 0, d], z_peer(d)
                )
        flush(len(copies))
        w = cw[it, 0, z]
        s_high, s_low = parts(spread_of(0, z, w))
        total = zs_c[it, 0, 0]
        for d in Z_ARRIVAL:
            copies[d].wait_recv()
            total = total + zr_c[it, 0, d]
        g_high, g_low = parts(total[:, CHUNK:])
        lower = nn(g_high, s_high) + (nn(g_high, s_low) + nn(g_low, s_high))
        cw[it + 1, 0, z] = w * total[:, 0:CHUNK] / lower
        if it < CHILD_ITERS - 1:
            ag_w = Spread(cw.at[it + 1], s_cw.at[it], r_cw.at[it])
        else:
            own_w = cw.at[it + 1, 0, z]
            copies = {
                d: send(own_w, own_w, s_cw.at[it, 0, d], r_cw.at[it, 0, d], z_peer(d)) for d in Z_SEND
            }

    outs = []

    def put(src, dst):
        copy = pltpu.make_async_copy(src, dst, out_sem.at[len(outs)])
        copy.start()
        outs.append(copy)

    def chunk_cols(zz):
        return pl.ds(pl.multiple_of(zz * CHUNK, CHUNK), CHUNK)

    put(hb.at[CHILD_ITERS], o_ch.at[:, own_cols])
    put(rh.at[ROOT_ITERS], o_rh.at[:, own_cols])
    rh_swap.wait_recv()
    put(rh_other, o_rh.at[:, other_cols])
    for i in range(ZN):
        put(rw.at[ROOT_ITERS, 0, i], o_rw.at[:, cols_of(i)])
    hb_swap.wait_recv()
    put(hb_other, o_ch.at[:, other_cols])
    put(own_w, o_cw.at[:, chunk_cols(z)])
    flush(0)
    for d in Z_ARRIVAL:
        copies[d].wait_recv()
        put(cw.at[CHILD_ITERS, 0, z_at(-d)], o_cw.at[:, chunk_cols(z_at(-d))])
    for out in outs:
        out.wait()


def put_out(*refs):
    sources, targets, held, sem = refs[:4], refs[4:8], refs[8:12], refs[12]
    loads = [pltpu.make_async_copy(s, h, sem.at[i]) for i, (s, h) in enumerate(zip(sources, held))]
    stores = [pltpu.make_async_copy(h, t, sem.at[4 + i]) for i, (h, t) in enumerate(zip(held, targets))]
    for load in loads:
        load.start()
    for load, store in zip(loads, stores):
        load.wait()
        store.start()
    for store in stores:
        store.wait()


def body(matrix, labels, root_rows, root_cols, child_rows, child_cols):
    vmem = pl.BlockSpec(memory_space=pltpu.VMEM)
    hbm = pl.BlockSpec(memory_space=pltpu.HBM)
    dma = pltpu.SemaphoreType.DMA
    r, c = ROOT_ITERS, CHILD_ITERS
    n = len(XY)

    def v(*shape, dtype=F32):
        return pltpu.VMEM(shape, dtype)

    i32 = jnp.int32
    scratch = [
        v(2, NODES, HALF, dtype=BF16), v(NODES, HALF, dtype=BF16), v(NODES, HALF), v(NODES, HALF),
        v(K_CHILD, HALF), v(1, NODES, dtype=i32), v(K_CHILD, NODES),
        v(2, ZN, K_CHILD, CHUNK, dtype=i32), v(2, ZN, K_CHILD, CHUNK),
        v(r + 1, K_ROOT, HALF), v(K_ROOT, HALF), v(r + 1, 2, ZN, K_ROOT, CHUNK),
        v(c + 1, 2, ZN, K_CHILD, CHUNK), v(c + 1, TOTAL, HALF), v(TOTAL, HALF),
        v(TOTAL, HALF, dtype=BF16), v(TOTAL, HALF), v(2 * TOTAL, 2 * K_CHILD),
        v(K_ROOT, HALF + 128), v(K_ROOT, HALF + 128), v(r, CHIPS, K_ROOT, HALF + 128),
        v(r, 2, ZN, K_ROOT, CHUNK + 128), v(r, 2, ZN, K_ROOT, CHUNK + 128),
        v(c, CHIPS, 8, HALF + 128), v(c, n, 8, HALF + 128),
        v(c, 2, ZN, K_CHILD, CHUNK + 128), v(c, 2, ZN, K_CHILD, CHUNK + 128),
        v(c, K_CHILD, TOTAL), v(c, K_CHILD, TOTAL),
        dma((10,)), dma((ZN,)), dma((ZN,)), dma((5,)), dma((5,)),
        dma((r, n)), dma((r, n)), dma((r, 2, ZN)), dma((r, 2, ZN)), dma((r, 2, ZN)), dma((r, 2, ZN)),
        dma((c, n)), dma((c, n)), dma((c, n)), dma((c, n)),
        dma((c, 2, ZN)), dma((c, 2, ZN)), dma((c, 2, ZN)), dma((c, 2, ZN)), dma((c,)), dma((c,)), dma((20,)),
    ]
    shapes = (
        jax.ShapeDtypeStruct((K_ROOT, NODES), F32),
        jax.ShapeDtypeStruct((K_ROOT, BINS), F32),
        jax.ShapeDtypeStruct((K_CHILD, NODES), F32),
        jax.ShapeDtypeStruct((TOTAL, BINS), F32),
    )
    outs = pl.pallas_call(
        kernel,
        out_shape=shapes,
        in_specs=[hbm, vmem, vmem, hbm, vmem, hbm],
        out_specs=(hbm,) * 4,
        scratch_shapes=scratch,
        compiler_params=pltpu.CompilerParams(
            collective_id=0, has_side_effects=True, vmem_limit_bytes=63 * 1024 * 1024
        ),
        name="nmf",
    )(matrix, labels.reshape(1, NODES), root_rows, root_cols, child_rows, child_cols)
    return pl.pallas_call(
        put_out,
        out_shape=shapes,
        in_specs=[hbm] * 4,
        out_specs=(hbm,) * 4,
        scratch_shapes=[v(*s.shape) for s in shapes] + [dma((8,))],
        compiler_params=pltpu.CompilerParams(vmem_limit_bytes=63 * 1024 * 1024),
        name="put_out",
    )(*outs)


def solution(mesh):
    return jax.shard_map(
        body,
        mesh=mesh,
        in_specs=(
            P("row", "col"), P("row", None), P(None, "row"),
            P(None, "col"), P(None, "row"), P(None, "col"),
        ),
        out_specs=(P(None, "row"), P(None, "col"), P(None, "row"), P(None, "col")),
        check_vma=False,
    )
```

```python
import jax
import jax.numpy as jnp
from jax import lax
from jax.experimental import pallas as pl
from jax.experimental.pallas import tpu as pltpu
from jax.sharding import PartitionSpec as P

MESH = pl.DeviceIdType.MESH
F32, BF16 = jnp.float32, jnp.bfloat16
K_ROOT, K_CHILD, CHILDREN = 8, 16, 8
ROOT_ITERS, CHILD_ITERS = 2, 3
TOTAL = CHILDREN * K_CHILD
NODES, BINS, HALF = 2048, 1024, 512
ZN, CHUNK = 8, 256
CHIPS = 16


def ring(d, n):
    return min(d, n - d)


XY = sorted(
    [(dx, dy) for dx in range(4) for dy in range(4) if dx or dy],
    key=lambda o: -(ring(o[0], 4) + ring(o[1], 4)),
)
XY_ARRIVAL = list(reversed(range(len(XY))))
Z_SEND = [4, 3, 5, 2, 6, 1, 7]
Z_ARRIVAL = [1, 7, 2, 6, 3, 5, 4]


def nn(a, b):
    return jnp.dot(a, b, preferred_element_type=F32)


def nt(a, b):
    return lax.dot_general(a, b, (((1,), (1,)), ((), ())), preferred_element_type=F32)


def parts(a):
    high = a.astype(BF16)
    return high, (a - high.astype(F32)).astype(BF16)


def gram3(high, low):
    return nt(high, high) + (nt(high, low) + nt(low, high))


def padded(gram):
    rows, cols = gram.shape
    return jnp.concatenate([gram, jnp.zeros((rows, 128 - cols), F32)], axis=1)


def small_product(gram, rows, count):
    total = gram[:, 0:1] * rows[0:1, :]
    for k in range(1, count):
        total = total + gram[:, k : k + 1] * rows[k : k + 1, :]
    return total


def kernel(
    x_hbm, lab_ref, rr_ref, rc_hbm, cr_ref, cc_hbm,
    o_rw, o_rh, o_cw, o_ch,
    xv, cc, lb, crv, rh, rw, cw, hb, hbb, acc, no, gacc,
    rxs, rxr, fr, zs_r, zr_r,
    nps, cxr, gxs, gxr, rss, rsr, zs_c, zr_c, gcs, gcr, ghs, ghr,
    in_sem, out_sem,
    s_rx, r_rx, s_fr, r_fr, s_rh, r_rh, s_zr, r_zr, s_rw, r_rw,
    s_cx, r_cx, s_rs, r_rs, s_ag, r_ag, s_re, r_re, s_zc, r_zc, s_cw, r_cw,
    s_gc, r_gc, s_gh, r_gh, s_gx, r_gx,
):
    row, z = lax.axis_index("row"), lax.axis_index("col")
    p, core = lax.div(row, 2), lax.rem(row, 2)
    x, y = lax.div(p, 4), lax.rem(p, 4)
    child = lax.div(p, 2)

    def chip(dx, dy):
        return lax.rem(x + dx + 4, 4) * 4 + lax.rem(y + dy + 4, 4)

    def xy_peer(o):
        return {"row": chip(*o) * 2 + core, "col": z}

    def z_at(d):
        return lax.rem(z + d + ZN, ZN)

    def z_peer(d):
        return {"row": row, "col": z_at(d)}

    partner = {"row": p * 2 + 1 - core, "col": z}
    pending = []

    def send(src, dst, ssem, rsem, device):
        copy = pltpu.make_async_remote_copy(
            src_ref=src, dst_ref=dst, send_sem=ssem, recv_sem=rsem,
            device_id=device, device_id_type=MESH,
        )
        copy.start()
        pending.append(copy)
        return copy

    def flush(keep):
        while len(pending) > keep:
            pending.pop(0).wait_send()

    loads = []
    for half in range(2):
        first = pl.multiple_of(HALF * (core if half == 0 else 1 - core), HALF)
        for i in range(4):
            rows = pl.ds(i * 512, 512)
            loads.append(
                pltpu.make_async_copy(
                    x_hbm.at[rows, pl.ds(first, HALF)], xv.at[half, rows], in_sem.at[half * 4 + i]
                )
            )
    own_cols = pl.ds(pl.multiple_of(HALF * core, HALF), HALF)
    other_cols = pl.ds(pl.multiple_of(HALF * (1 - core), HALF), HALF)
    load_cc = pltpu.make_async_copy(
        cc_hbm.at[pl.ds(pl.multiple_of(child * K_CHILD, 16), K_CHILD), own_cols], cc, in_sem.at[8]
    )
    load_rc = pltpu.make_async_copy(rc_hbm.at[:, own_cols], rh.at[0, 0], in_sem.at[9])
    for load in loads:
        load.start()
    load_rc.start()
    load_cc.start()

    barrier = pltpu.get_barrier_semaphore()
    pl.semaphore_signal(barrier, inc=1, device_id=partner, device_id_type=MESH)
    for o in XY:
        pl.semaphore_signal(barrier, inc=1, device_id=xy_peer(o), device_id_type=MESH)
    for d in Z_SEND:
        pl.semaphore_signal(barrier, inc=1, device_id=z_peer(d), device_id_type=MESH)

    for i in range(ZN):
        cols = slice(i * CHUNK, (i + 1) * CHUNK)
        rw[0, i] = rr_ref[:, cols]
        crv[i] = cr_ref[:, cols]
        lb[i] = jnp.broadcast_to(lab_ref[:, cols], (K_CHILD, CHUNK))

    def chunk_rows(zz):
        return pl.ds(zz * CHUNK if isinstance(zz, int) else pl.multiple_of(zz * CHUNK, CHUNK), CHUNK)

    def x_chunk(half, zz):
        return xv[half, chunk_rows(zz), :]

    ag_w = None
    for it in range(ROOT_ITERS):
        mine = other = gram = None
        for step, d in enumerate([0] + Z_ARRIVAL):
            if it == 0:
                zz = step
                if step % 2 == 0:
                    loads[step // 2].wait()
                    loads[4 + step // 2].wait()
            else:
                zz = z_at(-d)
                if d:
                    ag_w[d].wait_recv()
            w = rw[it, zz]
            high, low = parts(w)
            other_d = nn(high, x_chunk(1, zz))
            mine_d = nn(high, x_chunk(0, zz))
            gram_d = gram3(high, low)
            other = other_d if other is None else other + other_d
            mine = mine_d if mine is None else mine + mine_d
            gram = gram_d if gram is None else gram + gram_d
        gram = padded(gram)
        if it == 0:
            load_rc.wait()
            load_cc.wait()
            pl.semaphore_wait(barrier, 1 + len(XY) + len(Z_SEND))
        rxs[it, :, 0:HALF] = other
        rxs[it, :, HALF:] = gram
        swap = send(rxs.at[it], rxr.at[it], s_rx.at[it], r_rx.at[it], partner)
        flush(1)
        swap.wait_recv()
        fr[it, p, :, 0:HALF] = mine + rxr[it, :, 0:HALF]
        fr[it, p, :, HALF:] = gram + rxr[it, :, HALF:]
        copies = [
            send(fr.at[it, p], fr.at[it, p], s_fr.at[it, i], r_fr.at[it, i], xy_peer(o))
            for i, o in enumerate(XY)
        ]
        flush(len(copies))
        for i in XY_ARRIVAL:
            copies[i].wait_recv()
        total = fr[it, 0]
        for q in range(1, CHIPS):
            total = total + fr[it, q]
        h = rh[it, 0]
        lower = small_product(total[:, HALF : HALF + K_ROOT], h, K_ROOT)
        h = h * total[:, 0:HALF] / lower
        rh[it + 1, 0] = h
        swap = send(rh.at[it + 1, 0], rh.at[it + 1, 1], s_rh.at[it], r_rh.at[it], partner)
        flush(1)
        high, low = parts(h)
        owns = {d: nt(high, x_chunk(0, z_at(d))) for d in Z_SEND + [0]}
        gram = gram3(high, low)
        swap.wait_recv()
        high, low = parts(rh[it + 1, 1])
        gram = padded(gram + gram3(high, low))
        copies = {}
        for d in Z_SEND + [0]:
            zs_r[it, d, :, 0:CHUNK] = owns[d] + nt(high, x_chunk(1, z_at(d)))
            zs_r[it, d, :, CHUNK:] = gram
            if d:
                copies[d] = send(zs_r.at[it, d], zr_r.at[it, d], s_zr.at[it, d], r_zr.at[it, d], z_peer(d))
        flush(len(copies))
        total = zs_r[it, 0]
        for d in Z_ARRIVAL:
            copies[d].wait_recv()
            total = total + zr_r[it, d]
        w = rw[it, z]
        lower = small_product(total[:, CHUNK : CHUNK + K_ROOT], w, K_ROOT)
        rw[it + 1, z] = w * total[:, 0:CHUNK] / lower
        ag_w = {
            d: send(rw.at[it + 1, z], rw.at[it + 1, z], s_rw.at[it, d], r_rw.at[it, d], z_peer(d))
            for d in Z_SEND
        }

    own16 = pl.ds(pl.multiple_of(child * K_CHILD, 16), K_CHILD)
    own8 = pl.ds(pl.multiple_of(p * 8, 8), 8)
    hb[0, 0, own16, :] = cc[...] * rh[ROOT_ITERS, 0, pl.ds(child, 1), :]

    def spread_of(zz, w):
        label = lb[zz]
        return jnp.concatenate([jnp.where(label == c, w, 0.0) for c in range(CHILDREN)], axis=0)

    lane_child = lax.div(lax.broadcasted_iota(jnp.int32, (K_CHILD, TOTAL), 1), K_CHILD)

    def diagonal(full):
        out = jnp.where(lane_child == 0, full[0:K_CHILD], 0.0)
        for c in range(1, CHILDREN):
            out = out + jnp.where(lane_child == c, full[c * K_CHILD : (c + 1) * K_CHILD], 0.0)
        return out

    for it in range(CHILD_ITERS):
        order = [0] + Z_ARRIVAL
        for d in order:
            zz = z_at(-d)
            if d:
                ag_w[d].wait_recv()
            if it == 0:
                label = lb[zz, 0:K_ROOT]
                ids = lax.broadcasted_iota(jnp.int32, (K_ROOT, CHUNK), 0)
                own_weight = jnp.sum(jnp.where(label == ids, rw[ROOT_ITERS, zz], 0.0), axis=0, keepdims=True)
                w = crv[zz] * own_weight
                cw[0, zz] = w
            else:
                w = cw[it, zz]
            high, low = parts(spread_of(zz, w))
            first, last = d == 0, d == order[-1]
            numer = nn(high, x_chunk(1, zz))
            nps[it] = numer if first else nps[it] + numer
            if last:
                swap = send(nps.at[it], cxr.at[it], s_cx.at[it, 0], r_cx.at[it, 0], partner)
            gram = nt(jnp.concatenate([high, low], axis=0), jnp.concatenate(parts(w), axis=0))
            gram = gram if first else gacc[...] + gram
            if not last:
                gacc[...] = gram
            else:
                gcs[it] = padded(
                    gram[0:TOTAL, 0:K_CHILD] + (gram[0:TOTAL, K_CHILD:] + gram[TOTAL:, 0:K_CHILD])
                )
                gcopies = []
                for i, o in enumerate(XY):
                    rows = pl.ds(pl.multiple_of(chip(*o) * 8, 8), 8)
                    gcopies.append(
                        send(gcs.at[it, rows], gcr.at[it, i], s_gc.at[it, i], r_gc.at[it, i], xy_peer(o))
                    )
            numer = nn(high, x_chunk(0, zz))
            no[...] = numer if first else no[...] + numer
        flush(1 + len(gcopies))
        swap.wait_recv()
        copies = []
        for i, o in enumerate(XY):
            q = chip(*o)
            rows = pl.ds(pl.multiple_of(q * 8, 8), 8)
            rss[it, q] = no[rows, :] + cxr[it, rows, :]
            copies.append(send(rss.at[it, q], rsr.at[it, i], s_rs.at[it, i], r_rs.at[it, i], xy_peer(o)))
        total = no[own8, :] + cxr[it, own8, :]
        gram = gcs[it, own8, :]
        for i in XY_ARRIVAL:
            gcopies[i].wait_recv()
            gram = gram + gcr[it, i]
        gxs[it, 0] = gram
        swap_g = send(gxs.at[it, 0], gxr.at[it, 0], s_cx.at[it, 1], r_cx.at[it, 1], partner)
        flush(len(copies) + 1)
        swap_g.wait_recv()
        gram = gram + gxr[it, 0]
        old16 = hb[it, 0, own16, :]
        lower = small_product(gram[:, 0:K_CHILD], old16, K_CHILD)
        for i in XY_ARRIVAL:
            copies[i].wait_recv()
            total = total + rsr[it, i]
        hb[it + 1, 0, own8, :] = hb[it, 0, own8, :] * total / lower
        own_h = hb.at[it + 1, 0, own8]
        copies = [
            send(own_h, own_h, s_ag.at[it, i], r_ag.at[it, i], xy_peer(o)) for i, o in enumerate(XY)
        ]
        relays = [send(own_h, hb.at[it + 1, 1, own8], s_re.at[it, 15], r_re.at[it, 15], partner)]
        flush(len(copies) + 1)
        for i in XY_ARRIVAL:
            copies[i].wait_recv()
            dx, dy = XY[i]
            rows = pl.ds(pl.multiple_of(chip(-dx, -dy) * 8, 8), 8)
            relays.append(
                send(hb.at[it + 1, 0, rows], hb.at[it + 1, 1, rows], s_re.at[it, i], r_re.at[it, i], partner)
            )
        high, low = parts(hb[it + 1, 0])
        hbb[0] = high
        full = nt(jnp.concatenate([high, low], axis=0), high)
        ghs[it] = diagonal(full[0:TOTAL] + (full[TOTAL:] + full[TOTAL:].T))
        gcopies = {
            d: send(ghs.at[it], ghr.at[it, d], s_gh.at[it, d], r_gh.at[it, d], z_peer(d)) for d in Z_SEND
        }
        for d in Z_SEND + [0]:
            acc[d] = nt(hbb[0], x_chunk(0, z_at(d)))
        flush(len(relays) + len(gcopies))
        for relay in relays:
            relay.wait_recv()
        hbb[1] = hb[it + 1, 1].astype(BF16)
        copies = {}
        for d in Z_SEND + [0]:
            zz = z_at(d)
            label = lb[zz]
            rows_all = acc[d] + nt(hbb[1], x_chunk(1, zz))
            numer = jnp.where(label == 0, rows_all[0:K_CHILD], 0.0)
            for c in range(1, CHILDREN):
                numer = numer + jnp.where(label == c, rows_all[c * K_CHILD : (c + 1) * K_CHILD], 0.0)
            zs_c[it, d] = numer
            if d:
                copies[d] = send(zs_c.at[it, d], zr_c.at[it, d], s_zc.at[it, d], r_zc.at[it, d], z_peer(d))
        gram = ghs[it]
        for d in Z_ARRIVAL:
            gcopies[d].wait_recv()
            gram = gram + ghr[it, d]
        gxs[it, 1:3] = gram.reshape(2, 8, TOTAL)
        swap_g = send(gxs.at[it, 1:3], gxr.at[it, 1:3], s_gx.at[it], r_gx.at[it], partner)
        flush(len(copies) + 1)
        w = cw[it, z]
        s_high, s_low = parts(spread_of(z, w))
        swap_g.wait_recv()
        g_high, g_low = parts(gram + gxr[it, 1:3].reshape(K_CHILD, TOTAL))
        lower = nn(g_high, s_high) + (nn(g_high, s_low) + nn(g_low, s_high))
        total = zs_c[it, 0]
        for d in Z_ARRIVAL:
            copies[d].wait_recv()
            total = total + zr_c[it, d]
        cw[it + 1, z] = w * total / lower
        ag_w = {
            d: send(cw.at[it + 1, z], cw.at[it + 1, z], s_cw.at[it, d], r_cw.at[it, d], z_peer(d))
            for d in Z_SEND
        }

    outs = []

    def put(src, dst):
        copy = pltpu.make_async_copy(src, dst, out_sem.at[len(outs)])
        copy.start()
        outs.append(copy)

    put(hb.at[CHILD_ITERS, 0], o_ch.at[:, own_cols])
    put(hb.at[CHILD_ITERS, 1], o_ch.at[:, other_cols])
    put(rh.at[ROOT_ITERS, 0], o_rh.at[:, own_cols])
    put(rh.at[ROOT_ITERS, 1], o_rh.at[:, other_cols])
    for i in range(ZN):
        put(rw.at[ROOT_ITERS, i], o_rw.at[:, i * CHUNK : (i + 1) * CHUNK])
    put(cw.at[CHILD_ITERS, z], o_cw.at[:, chunk_rows(z)])
    flush(0)
    for d in Z_ARRIVAL:
        ag_w[d].wait_recv()
        put(cw.at[CHILD_ITERS, z_at(-d)], o_cw.at[:, chunk_rows(z_at(-d))])
    for out in outs:
        out.wait()


def put_out(*refs):
    sources, targets, held, sem = refs[:4], refs[4:8], refs[8:12], refs[12]
    loads = [pltpu.make_async_copy(s, h, sem.at[i]) for i, (s, h) in enumerate(zip(sources, held))]
    stores = [pltpu.make_async_copy(h, t, sem.at[4 + i]) for i, (h, t) in enumerate(zip(held, targets))]
    for load in loads:
        load.start()
    for load, store in zip(loads, stores):
        load.wait()
        store.start()
    for store in stores:
        store.wait()


def body(matrix, labels, root_rows, root_cols, child_rows, child_cols):
    vmem = pl.BlockSpec(memory_space=pltpu.VMEM)
    hbm = pl.BlockSpec(memory_space=pl.ANY)
    dma = pltpu.SemaphoreType.DMA
    r, c = ROOT_ITERS, CHILD_ITERS
    n = len(XY)

    def v(*shape, dtype=F32):
        return pltpu.VMEM(shape, dtype)

    scratch = [
        v(2, NODES, HALF, dtype=BF16), v(K_CHILD, HALF), v(ZN, K_CHILD, CHUNK, dtype=jnp.int32),
        v(ZN, K_CHILD, CHUNK), v(r + 1, 2, K_ROOT, HALF), v(r + 1, ZN, K_ROOT, CHUNK),
        v(c + 1, ZN, K_CHILD, CHUNK), v(c + 1, 2, TOTAL, HALF), v(2, TOTAL, HALF, dtype=BF16),
        v(ZN, TOTAL, CHUNK), v(TOTAL, HALF), v(2 * TOTAL, 2 * K_CHILD),
        v(r, K_ROOT, HALF + 128), v(r, K_ROOT, HALF + 128), v(r, CHIPS, K_ROOT, HALF + 128),
        v(r, ZN, K_ROOT, CHUNK + 128), v(r, ZN, K_ROOT, CHUNK + 128),
        v(c, TOTAL, HALF), v(c, TOTAL, HALF), v(c, 3, 8, TOTAL), v(c, 3, 8, TOTAL),
        v(c, CHIPS, 8, HALF), v(c, n, 8, HALF),
        v(c, ZN, K_CHILD, CHUNK), v(c, ZN, K_CHILD, CHUNK),
        v(c, TOTAL, 128), v(c, n, 8, 128), v(c, K_CHILD, TOTAL), v(c, ZN, K_CHILD, TOTAL),
        dma((10,)), dma((20,)),
        dma((r,)), dma((r,)), dma((r, n)), dma((r, n)), dma((r,)), dma((r,)),
        dma((r, ZN)), dma((r, ZN)), dma((r, ZN)), dma((r, ZN)),
        dma((c, 2)), dma((c, 2)), dma((c, n)), dma((c, n)), dma((c, n)), dma((c, n)),
        dma((c, n + 1)), dma((c, n + 1)), dma((c, ZN)), dma((c, ZN)), dma((c, ZN)), dma((c, ZN)),
        dma((c, n)), dma((c, n)), dma((c, ZN)), dma((c, ZN)), dma((c,)), dma((c,)),
    ]
    shapes = (
        jax.ShapeDtypeStruct((K_ROOT, NODES), F32),
        jax.ShapeDtypeStruct((K_ROOT, BINS), F32),
        jax.ShapeDtypeStruct((K_CHILD, NODES), F32),
        jax.ShapeDtypeStruct((TOTAL, BINS), F32),
    )
    outs = pl.pallas_call(
        kernel,
        out_shape=shapes,
        in_specs=[hbm, vmem, vmem, hbm, vmem, hbm],
        out_specs=(hbm,) * 4,
        scratch_shapes=scratch,
        compiler_params=pltpu.CompilerParams(
            collective_id=0, has_side_effects=True, vmem_limit_bytes=63 * 1024 * 1024
        ),
        name="nmf",
    )(matrix, labels.reshape(1, NODES), root_rows, root_cols, child_rows, child_cols)
    return pl.pallas_call(
        put_out,
        out_shape=shapes,
        in_specs=[hbm] * 4,
        out_specs=(hbm,) * 4,
        scratch_shapes=[v(*s.shape) for s in shapes] + [dma((8,))],
        compiler_params=pltpu.CompilerParams(vmem_limit_bytes=63 * 1024 * 1024),
        name="put_out",
    )(*outs)


def solution(mesh):
    return jax.shard_map(
        body,
        mesh=mesh,
        in_specs=(
            P("row", "col"), P("row", None), P(None, "row"),
            P(None, "col"), P(None, "row"), P(None, "col"),
        ),
        out_specs=(P(None, "row"), P(None, "col"), P(None, "row"), P(None, "col")),
        check_vma=False,
    )
```

```python
import jax
import jax.numpy as jnp
from jax import lax
from jax.experimental import pallas as pl
from jax.experimental.pallas import tpu as pltpu
from jax.sharding import PartitionSpec as P

MESH = pl.DeviceIdType.MESH
F32, BF16 = jnp.float32, jnp.bfloat16
K_ROOT, K_CHILD, CHILDREN = 8, 16, 8
ROOT_ITERS, CHILD_ITERS = 2, 3
TOTAL = CHILDREN * K_CHILD
NODES, BINS, HALF = 2048, 1024, 512
ZN, CHUNK = 8, 256
CHIPS = 16


def ring(d, n):
    return min(d, n - d)


XY = sorted(
    [(dx, dy) for dx in range(4) for dy in range(4) if dx or dy],
    key=lambda o: -(ring(o[0], 4) + ring(o[1], 4)),
)
XY_ARRIVAL = list(reversed(range(len(XY))))
Z_SEND = [4, 3, 5, 2, 6, 1, 7]
Z_ARRIVAL = [1, 7, 2, 6, 3, 5, 4]
Z_GROUPS = [[0], [1, 7], [2, 6], [3, 5], [4]]


def nn(a, b):
    return jnp.dot(a, b, preferred_element_type=F32)


def nt(a, b):
    return lax.dot_general(a, b, (((1,), (1,)), ((), ())), preferred_element_type=F32)


def parts(a):
    high = a.astype(BF16)
    return high, (a - high.astype(F32)).astype(BF16)


def gram3(high, low):
    return nt(high, high) + (nt(high, low) + nt(low, high))


def padded(gram):
    rows, cols = gram.shape
    return jnp.concatenate([gram, jnp.zeros((rows, 128 - cols), F32)], axis=1)


def plus(a, b):
    return b if a is None else a + b


def small_product(gram, rows, count):
    total = gram[:, 0:1] * rows[0:1, :]
    for k in range(1, count):
        total = total + gram[:, k : k + 1] * rows[k : k + 1, :]
    return total


def kernel(
    x_hbm, lab_ref, rr_ref, rc_hbm, cr_ref, cc_hbm,
    o_rw, o_rh, o_cw, o_ch,
    xv, cc, lb, crv, rh, rw, cw, hb, hbb, acc, no, gacc,
    rxs, rxr, fr, gfr, gfs, gft, zs_r, zr_r,
    nps, cxr, gxs, gxr, rss, rsr, zs_c, zr_c, gcs, gcr, ghs, ghr,
    in_sem, out_sem,
    s_rx, r_rx, s_fr, r_fr, s_rh, r_rh, s_zr, r_zr, s_rw, r_rw,
    s_cx, r_cx, s_rs, r_rs, s_ag, r_ag, s_re, r_re, s_zc, r_zc, s_cw, r_cw,
    s_gc, r_gc, s_gh, r_gh, s_gx, r_gx, s_gf, r_gf, s_gt, r_gt,
):
    row, z = lax.axis_index("row"), lax.axis_index("col")
    p, core = lax.div(row, 2), lax.rem(row, 2)
    x, y = lax.div(p, 4), lax.rem(p, 4)
    child = lax.div(p, 2)

    def chip(dx, dy):
        return lax.rem(x + dx + 4, 4) * 4 + lax.rem(y + dy + 4, 4)

    def xy_peer(o):
        return {"row": chip(*o) * 2 + core, "col": z}

    def z_at(d):
        return lax.rem(z + d + ZN, ZN)

    def z_peer(d):
        return {"row": row, "col": z_at(d)}

    partner = {"row": p * 2 + 1 - core, "col": z}
    pending = []

    def send(src, dst, ssem, rsem, device):
        copy = pltpu.make_async_remote_copy(
            src_ref=src, dst_ref=dst, send_sem=ssem, recv_sem=rsem,
            device_id=device, device_id_type=MESH,
        )
        copy.start()
        pending.append(copy)
        return copy

    def flush():
        while pending:
            pending.pop(0).wait_send()

    loads = []
    for half in range(2):
        first = pl.multiple_of(HALF * (core if half == 0 else 1 - core), HALF)
        for i in range(4):
            rows = pl.ds(i * 512, 512)
            loads.append(
                pltpu.make_async_copy(
                    x_hbm.at[rows, pl.ds(first, HALF)], xv.at[half, rows], in_sem.at[half * 4 + i]
                )
            )
    own_cols = pl.ds(pl.multiple_of(HALF * core, HALF), HALF)
    other_cols = pl.ds(pl.multiple_of(HALF * (1 - core), HALF), HALF)
    load_cc = pltpu.make_async_copy(
        cc_hbm.at[pl.ds(pl.multiple_of(child * K_CHILD, 16), K_CHILD), own_cols], cc, in_sem.at[8]
    )
    load_rc = pltpu.make_async_copy(rc_hbm.at[:, own_cols], rh.at[0, 0], in_sem.at[9])
    for load in loads:
        load.start()
    load_rc.start()
    load_cc.start()

    barrier = pltpu.get_barrier_semaphore()
    pl.semaphore_signal(barrier, inc=1, device_id=partner, device_id_type=MESH)
    for o in XY:
        pl.semaphore_signal(barrier, inc=1, device_id=xy_peer(o), device_id_type=MESH)
    for d in Z_SEND:
        pl.semaphore_signal(barrier, inc=1, device_id=z_peer(d), device_id_type=MESH)

    for i in range(ZN):
        cols = slice(i * CHUNK, (i + 1) * CHUNK)
        rw[0, i] = rr_ref[:, cols]
        crv[i] = cr_ref[:, cols]
        lb[i] = jnp.broadcast_to(lab_ref[:, cols], (K_CHILD, CHUNK))

    def chunk_rows(zz):
        return pl.ds(zz * CHUNK if isinstance(zz, int) else pl.multiple_of(zz * CHUNK, CHUNK), CHUNK)

    def x_chunk(half, zz):
        return xv[half, chunk_rows(zz), :]

    def x_rows(half, places):
        return jnp.concatenate([x_chunk(half, zz) for zz in places], axis=0)

    ag_w = None
    for it in range(ROOT_ITERS):
        mine = other = gram = None
        for step, group in enumerate([[2 * i, 2 * i + 1] for i in range(4)] if it == 0 else Z_GROUPS):
            places = []
            for d in group:
                if it == 0:
                    places.append(d)
                else:
                    if d:
                        ag_w[d].wait_recv()
                    places.append(z_at(-d))
            if it == 0:
                loads[step].wait()
                loads[4 + step].wait()
            w = jnp.concatenate([rw[it, zz] for zz in places], axis=1)
            high, low = parts(w)
            other = plus(other, nn(high, x_rows(1, places)))
            mine = plus(mine, nn(high, x_rows(0, places)))
            gram = plus(gram, gram3(high, low))
        if it == 0:
            load_rc.wait()
            load_cc.wait()
            pl.semaphore_wait(barrier, 1 + len(XY) + len(Z_SEND))
        rxs[it] = other
        swap = send(rxs.at[it], rxr.at[it], s_rx.at[it], r_rx.at[it], partner)
        own_g = gfr.at[it, p]
        gfr[it, p] = padded(gram)
        gcopies = [
            send(own_g, own_g, s_gf.at[it, i], r_gf.at[it, i], xy_peer(o)) for i, o in enumerate(XY)
        ]
        swap.wait_recv()
        fr[it, p] = mine + rxr[it]
        copies = [
            send(fr.at[it, p], fr.at[it, p], s_fr.at[it, i], r_fr.at[it, i], xy_peer(o))
            for i, o in enumerate(XY)
        ]
        for i in XY_ARRIVAL:
            gcopies[i].wait_recv()
        gram = gfr[it, 0]
        for q in range(1, CHIPS):
            gram = gram + gfr[it, q]
        gfs[it] = gram
        swap = send(gfs.at[it], gft.at[it], s_gt.at[it], r_gt.at[it], partner)
        swap.wait_recv()
        gram = gram + gft[it]
        lower = small_product(gram[:, 0:K_ROOT], rh[it, 0], K_ROOT)
        for i in XY_ARRIVAL:
            copies[i].wait_recv()
        total = fr[it, 0]
        for q in range(1, CHIPS):
            total = total + fr[it, q]
        h = rh[it, 0] * total / lower
        rh[it + 1, 0] = h
        swap = send(rh.at[it + 1, 0], rh.at[it + 1, 1], s_rh.at[it], r_rh.at[it], partner)
        high, low = parts(h)
        owns = {d: nt(high, x_chunk(0, z_at(d))) for d in Z_SEND + [0]}
        gram = gram3(high, low)
        swap.wait_recv()
        high, low = parts(rh[it + 1, 1])
        gram = padded(gram + gram3(high, low))
        copies = {}
        for d in Z_SEND + [0]:
            zs_r[it, d, :, 0:CHUNK] = owns[d] + nt(high, x_chunk(1, z_at(d)))
            zs_r[it, d, :, CHUNK:] = gram
            if d:
                copies[d] = send(zs_r.at[it, d], zr_r.at[it, d], s_zr.at[it, d], r_zr.at[it, d], z_peer(d))
        total = zs_r[it, 0]
        for d in Z_ARRIVAL:
            copies[d].wait_recv()
            total = total + zr_r[it, d]
        w = rw[it, z]
        lower = small_product(total[:, CHUNK : CHUNK + K_ROOT], w, K_ROOT)
        rw[it + 1, z] = w * total[:, 0:CHUNK] / lower
        ag_w = {
            d: send(rw.at[it + 1, z], rw.at[it + 1, z], s_rw.at[it, d], r_rw.at[it, d], z_peer(d))
            for d in Z_SEND
        }

    own16 = pl.ds(pl.multiple_of(child * K_CHILD, 16), K_CHILD)
    own8 = pl.ds(pl.multiple_of(p * 8, 8), 8)
    hb[0, 0, own16, :] = cc[...] * rh[ROOT_ITERS, 0, pl.ds(child, 1), :]

    def spread_of(zz, w):
        label = lb[zz]
        return jnp.concatenate([jnp.where(label == c, w, 0.0) for c in range(CHILDREN)], axis=0)

    lane_child = lax.div(lax.broadcasted_iota(jnp.int32, (K_CHILD, TOTAL), 1), K_CHILD)

    def diagonal(full):
        out = jnp.where(lane_child == 0, full[0:K_CHILD], 0.0)
        for c in range(1, CHILDREN):
            out = out + jnp.where(lane_child == c, full[c * K_CHILD : (c + 1) * K_CHILD], 0.0)
        return out

    for it in range(CHILD_ITERS):
        for group in Z_GROUPS:
            places, ws, spreads = [], [], []
            for d in group:
                zz = z_at(-d)
                if d:
                    ag_w[d].wait_recv()
                if it == 0:
                    label = lb[zz, 0:K_ROOT]
                    ids = lax.broadcasted_iota(jnp.int32, (K_ROOT, CHUNK), 0)
                    own_weight = jnp.sum(
                        jnp.where(label == ids, rw[ROOT_ITERS, zz], 0.0), axis=0, keepdims=True
                    )
                    w = crv[zz] * own_weight
                    cw[0, zz] = w
                else:
                    w = cw[it, zz]
                places.append(zz)
                ws.append(w)
                spreads.append(spread_of(zz, w))
            high, low = parts(jnp.concatenate(spreads, axis=1))
            w = jnp.concatenate(ws, axis=1)
            first, last = group is Z_GROUPS[0], group is Z_GROUPS[-1]
            numer = nn(high, x_rows(1, places))
            nps[it] = numer if first else nps[it] + numer
            if last:
                swap = send(nps.at[it], cxr.at[it], s_cx.at[it, 0], r_cx.at[it, 0], partner)
            gram = nt(jnp.concatenate([high, low], axis=0), jnp.concatenate(parts(w), axis=0))
            gram = gram if first else gacc[...] + gram
            if not last:
                gacc[...] = gram
            else:
                gcs[it] = padded(
                    gram[0:TOTAL, 0:K_CHILD] + (gram[0:TOTAL, K_CHILD:] + gram[TOTAL:, 0:K_CHILD])
                )
                gcopies = []
                for i, o in enumerate(XY):
                    rows = pl.ds(pl.multiple_of(chip(*o) * 8, 8), 8)
                    gcopies.append(
                        send(gcs.at[it, rows], gcr.at[it, i], s_gc.at[it, i], r_gc.at[it, i], xy_peer(o))
                    )
            numer = nn(high, x_rows(0, places))
            no[...] = numer if first else no[...] + numer
        swap.wait_recv()
        copies = []
        for i, o in enumerate(XY):
            q = chip(*o)
            rows = pl.ds(pl.multiple_of(q * 8, 8), 8)
            rss[it, q] = no[rows, :] + cxr[it, rows, :]
            copies.append(send(rss.at[it, q], rsr.at[it, i], s_rs.at[it, i], r_rs.at[it, i], xy_peer(o)))
        total = no[own8, :] + cxr[it, own8, :]
        gram = gcs[it, own8, :]
        for i in XY_ARRIVAL:
            gcopies[i].wait_recv()
            gram = gram + gcr[it, i]
        gxs[it, 0] = gram
        swap_g = send(gxs.at[it, 0], gxr.at[it, 0], s_cx.at[it, 1], r_cx.at[it, 1], partner)
        swap_g.wait_recv()
        gram = gram + gxr[it, 0]
        old16 = hb[it, 0, own16, :]
        lower = small_product(gram[:, 0:K_CHILD], old16, K_CHILD)
        for i in XY_ARRIVAL:
            copies[i].wait_recv()
            total = total + rsr[it, i]
        hb[it + 1, 0, own8, :] = hb[it, 0, own8, :] * total / lower
        own_h = hb.at[it + 1, 0, own8]
        copies = [
            send(own_h, own_h, s_ag.at[it, i], r_ag.at[it, i], xy_peer(o)) for i, o in enumerate(XY)
        ]
        relays = [send(own_h, hb.at[it + 1, 1, own8], s_re.at[it, 15], r_re.at[it, 15], partner)]
        for i in XY_ARRIVAL:
            copies[i].wait_recv()
            dx, dy = XY[i]
            rows = pl.ds(pl.multiple_of(chip(-dx, -dy) * 8, 8), 8)
            relays.append(
                send(hb.at[it + 1, 0, rows], hb.at[it + 1, 1, rows], s_re.at[it, i], r_re.at[it, i], partner)
            )
        high, low = parts(hb[it + 1, 0])
        hbb[0] = high
        full = nt(jnp.concatenate([high, low], axis=0), high)
        ghs[it] = diagonal(full[0:TOTAL] + (full[TOTAL:] + full[TOTAL:].T))
        gcopies = {
            d: send(ghs.at[it], ghr.at[it, d], s_gh.at[it, d], r_gh.at[it, d], z_peer(d)) for d in Z_SEND
        }
        for d in Z_SEND + [0]:
            acc[d] = nt(hbb[0], x_chunk(0, z_at(d)))
        for relay in relays:
            relay.wait_recv()
        hbb[1] = hb[it + 1, 1].astype(BF16)
        copies = {}
        for d in Z_SEND + [0]:
            zz = z_at(d)
            label = lb[zz]
            rows_all = acc[d] + nt(hbb[1], x_chunk(1, zz))
            numer = jnp.where(label == 0, rows_all[0:K_CHILD], 0.0)
            for c in range(1, CHILDREN):
                numer = numer + jnp.where(label == c, rows_all[c * K_CHILD : (c + 1) * K_CHILD], 0.0)
            zs_c[it, d] = numer
            if d:
                copies[d] = send(zs_c.at[it, d], zr_c.at[it, d], s_zc.at[it, d], r_zc.at[it, d], z_peer(d))
        gram = ghs[it]
        for d in Z_ARRIVAL:
            gcopies[d].wait_recv()
            gram = gram + ghr[it, d]
        gxs[it, 1:3] = gram.reshape(2, 8, TOTAL)
        swap_g = send(gxs.at[it, 1:3], gxr.at[it, 1:3], s_gx.at[it], r_gx.at[it], partner)
        w = cw[it, z]
        s_high, s_low = parts(spread_of(z, w))
        swap_g.wait_recv()
        g_high, g_low = parts(gram + gxr[it, 1:3].reshape(K_CHILD, TOTAL))
        lower = nn(g_high, s_high) + (nn(g_high, s_low) + nn(g_low, s_high))
        total = zs_c[it, 0]
        for d in Z_ARRIVAL:
            copies[d].wait_recv()
            total = total + zr_c[it, d]
        cw[it + 1, z] = w * total / lower
        ag_w = {
            d: send(cw.at[it + 1, z], cw.at[it + 1, z], s_cw.at[it, d], r_cw.at[it, d], z_peer(d))
            for d in Z_SEND
        }

    outs = []

    def put(src, dst):
        copy = pltpu.make_async_copy(src, dst, out_sem.at[len(outs)])
        copy.start()
        outs.append(copy)

    put(hb.at[CHILD_ITERS, 0], o_ch.at[:, own_cols])
    put(hb.at[CHILD_ITERS, 1], o_ch.at[:, other_cols])
    put(rh.at[ROOT_ITERS, 0], o_rh.at[:, own_cols])
    put(rh.at[ROOT_ITERS, 1], o_rh.at[:, other_cols])
    for i in range(ZN):
        put(rw.at[ROOT_ITERS, i], o_rw.at[:, i * CHUNK : (i + 1) * CHUNK])
    put(cw.at[CHILD_ITERS, z], o_cw.at[:, chunk_rows(z)])
    flush()
    for d in Z_ARRIVAL:
        ag_w[d].wait_recv()
        put(cw.at[CHILD_ITERS, z_at(-d)], o_cw.at[:, chunk_rows(z_at(-d))])
    for out in outs:
        out.wait()


def put_out(*refs):
    sources, targets, held, sem = refs[:4], refs[4:8], refs[8:12], refs[12]
    loads = [pltpu.make_async_copy(s, h, sem.at[i]) for i, (s, h) in enumerate(zip(sources, held))]
    stores = [pltpu.make_async_copy(h, t, sem.at[4 + i]) for i, (h, t) in enumerate(zip(held, targets))]
    for load in loads:
        load.start()
    for load, store in zip(loads, stores):
        load.wait()
        store.start()
    for store in stores:
        store.wait()


def body(matrix, labels, root_rows, root_cols, child_rows, child_cols):
    vmem = pl.BlockSpec(memory_space=pltpu.VMEM)
    hbm = pl.BlockSpec(memory_space=pl.ANY)
    dma = pltpu.SemaphoreType.DMA
    r, c = ROOT_ITERS, CHILD_ITERS
    n = len(XY)

    def v(*shape, dtype=F32):
        return pltpu.VMEM(shape, dtype)

    scratch = [
        v(2, NODES, HALF, dtype=BF16), v(K_CHILD, HALF), v(ZN, K_CHILD, CHUNK, dtype=jnp.int32),
        v(ZN, K_CHILD, CHUNK), v(r + 1, 2, K_ROOT, HALF), v(r + 1, ZN, K_ROOT, CHUNK),
        v(c + 1, ZN, K_CHILD, CHUNK), v(c + 1, 2, TOTAL, HALF), v(2, TOTAL, HALF, dtype=BF16),
        v(ZN, TOTAL, CHUNK), v(TOTAL, HALF), v(2 * TOTAL, 2 * K_CHILD),
        v(r, K_ROOT, HALF), v(r, K_ROOT, HALF), v(r, CHIPS, K_ROOT, HALF),
        v(r, CHIPS, K_ROOT, 128), v(r, K_ROOT, 128), v(r, K_ROOT, 128),
        v(r, ZN, K_ROOT, CHUNK + 128), v(r, ZN, K_ROOT, CHUNK + 128),
        v(c, TOTAL, HALF), v(c, TOTAL, HALF), v(c, 3, 8, TOTAL), v(c, 3, 8, TOTAL),
        v(c, CHIPS, 8, HALF), v(c, n, 8, HALF),
        v(c, ZN, K_CHILD, CHUNK), v(c, ZN, K_CHILD, CHUNK),
        v(c, TOTAL, 128), v(c, n, 8, 128), v(c, K_CHILD, TOTAL), v(c, ZN, K_CHILD, TOTAL),
        dma((10,)), dma((20,)),
        dma((r,)), dma((r,)), dma((r, n)), dma((r, n)), dma((r,)), dma((r,)),
        dma((r, ZN)), dma((r, ZN)), dma((r, ZN)), dma((r, ZN)),
        dma((c, 2)), dma((c, 2)), dma((c, n)), dma((c, n)), dma((c, n)), dma((c, n)),
        dma((c, n + 1)), dma((c, n + 1)), dma((c, ZN)), dma((c, ZN)), dma((c, ZN)), dma((c, ZN)),
        dma((c, n)), dma((c, n)), dma((c, ZN)), dma((c, ZN)), dma((c,)), dma((c,)),
        dma((r, n)), dma((r, n)), dma((r,)), dma((r,)),
    ]
    shapes = (
        jax.ShapeDtypeStruct((K_ROOT, NODES), F32),
        jax.ShapeDtypeStruct((K_ROOT, BINS), F32),
        jax.ShapeDtypeStruct((K_CHILD, NODES), F32),
        jax.ShapeDtypeStruct((TOTAL, BINS), F32),
    )
    outs = pl.pallas_call(
        kernel,
        out_shape=shapes,
        in_specs=[hbm, vmem, vmem, hbm, vmem, hbm],
        out_specs=(hbm,) * 4,
        scratch_shapes=scratch,
        compiler_params=pltpu.CompilerParams(
            collective_id=0, has_side_effects=True, vmem_limit_bytes=63 * 1024 * 1024
        ),
        name="nmf",
    )(matrix, labels.reshape(1, NODES), root_rows, root_cols, child_rows, child_cols)
    return pl.pallas_call(
        put_out,
        out_shape=shapes,
        in_specs=[hbm] * 4,
        out_specs=(hbm,) * 4,
        scratch_shapes=[v(*s.shape) for s in shapes] + [dma((8,))],
        compiler_params=pltpu.CompilerParams(vmem_limit_bytes=63 * 1024 * 1024),
        name="put_out",
    )(*outs)


def solution(mesh):
    return jax.shard_map(
        body,
        mesh=mesh,
        in_specs=(
            P("row", "col"), P("row", None), P(None, "row"),
            P(None, "col"), P(None, "row"), P(None, "col"),
        ),
        out_specs=(P(None, "row"), P(None, "col"), P(None, "row"), P(None, "col")),
        check_vma=False,
    )
```

```python
import jax
import jax.numpy as jnp
from jax import lax
from jax.experimental import pallas as pl
from jax.experimental.pallas import tpu as pltpu
from jax.sharding import PartitionSpec as P

MESH = pl.DeviceIdType.MESH
F32, BF16 = jnp.float32, jnp.bfloat16
K_ROOT, K_CHILD, CHILDREN = 8, 16, 8
ROOT_ITERS, CHILD_ITERS = 2, 3
TOTAL = CHILDREN * K_CHILD
NODES, BINS, HALF = 2048, 1024, 512
ZN, CHUNK = 8, 256
CHIPS = 16


def ring(d, n):
    return min(d, n - d)


XY = sorted(
    [(dx, dy) for dx in range(4) for dy in range(4) if dx or dy],
    key=lambda o: -(ring(o[0], 4) + ring(o[1], 4)),
)
XY_ARRIVAL = list(reversed(range(len(XY))))
Z_SEND = [4, 3, 5, 2, 6, 1, 7]
Z_ARRIVAL = [1, 7, 2, 6, 3, 5, 4]
Z_GROUPS = [[0], [1, 7], [2, 6], [3, 5], [4]]


def nn(a, b):
    return jnp.dot(a, b, preferred_element_type=F32)


def nt(a, b):
    return lax.dot_general(a, b, (((1,), (1,)), ((), ())), preferred_element_type=F32)


def parts(a):
    high = a.astype(BF16)
    return high, (a - high.astype(F32)).astype(BF16)


def gram3(high, low):
    return nt(high, high) + (nt(high, low) + nt(low, high))


def padded(gram):
    rows, cols = gram.shape
    return jnp.concatenate([gram, jnp.zeros((rows, 128 - cols), F32)], axis=1)


def plus(a, b):
    return b if a is None else a + b


def small_product(gram, rows, count):
    total = gram[:, 0:1] * rows[0:1, :]
    for k in range(1, count):
        total = total + gram[:, k : k + 1] * rows[k : k + 1, :]
    return total


def kernel(
    x_hbm, lab_ref, rr_ref, rc_hbm, cr_ref, cc_hbm,
    o_rw, o_rh, o_cw, o_ch,
    xv, cc, lb, crv, rh, rw, cw, hb, hbb, acc, no, gacc,
    rxs, rxr, fr, gfr, gfs, gft, ghr_own, ghr_in, gzs, gzt, zs_r, zr_r,
    nps, cxr, gxs, gxr, rss, rsr, zs_c, zr_c, gcs, gcr, ghs, ghr,
    in_sem, out_sem,
    s_rx, r_rx, s_fr, r_fr, s_rh, r_rh, s_zr, r_zr, s_rw, r_rw,
    s_cx, r_cx, s_rs, r_rs, s_ag, r_ag, s_re, r_re, s_zc, r_zc, s_cw, r_cw,
    s_gc, r_gc, s_gh, r_gh, s_gx, r_gx, s_gf, r_gf, s_gt, r_gt, s_gz, r_gz,
):
    row, z = lax.axis_index("row"), lax.axis_index("col")
    p, core = lax.div(row, 2), lax.rem(row, 2)
    x, y = lax.div(p, 4), lax.rem(p, 4)
    child = lax.div(p, 2)

    def chip(dx, dy):
        return lax.rem(x + dx + 4, 4) * 4 + lax.rem(y + dy + 4, 4)

    def xy_peer(o):
        return {"row": chip(*o) * 2 + core, "col": z}

    def z_at(d):
        return lax.rem(z + d + ZN, ZN)

    def z_peer(d):
        return {"row": row, "col": z_at(d)}

    partner = {"row": p * 2 + 1 - core, "col": z}
    pending = []

    def send(src, dst, ssem, rsem, device):
        copy = pltpu.make_async_remote_copy(
            src_ref=src, dst_ref=dst, send_sem=ssem, recv_sem=rsem,
            device_id=device, device_id_type=MESH,
        )
        copy.start()
        pending.append(copy)
        return copy

    def flush():
        while pending:
            pending.pop(0).wait_send()

    loads = []
    for half in range(2):
        first = pl.multiple_of(HALF * (core if half == 0 else 1 - core), HALF)
        for i in range(4):
            rows = pl.ds(i * 512, 512)
            loads.append(
                pltpu.make_async_copy(
                    x_hbm.at[rows, pl.ds(first, HALF)], xv.at[half, rows], in_sem.at[half * 4 + i]
                )
            )
    own_cols = pl.ds(pl.multiple_of(HALF * core, HALF), HALF)
    other_cols = pl.ds(pl.multiple_of(HALF * (1 - core), HALF), HALF)
    load_cc = pltpu.make_async_copy(
        cc_hbm.at[pl.ds(pl.multiple_of(child * K_CHILD, 16), K_CHILD), own_cols], cc, in_sem.at[8]
    )
    load_rc = pltpu.make_async_copy(rc_hbm.at[:, own_cols], rh.at[0, 0], in_sem.at[9])
    for load in loads:
        load.start()
    load_rc.start()
    load_cc.start()

    barrier = pltpu.get_barrier_semaphore()
    pl.semaphore_signal(barrier, inc=1, device_id=partner, device_id_type=MESH)
    for o in XY:
        pl.semaphore_signal(barrier, inc=1, device_id=xy_peer(o), device_id_type=MESH)
    for d in Z_SEND:
        pl.semaphore_signal(barrier, inc=1, device_id=z_peer(d), device_id_type=MESH)

    for i in range(ZN):
        cols = slice(i * CHUNK, (i + 1) * CHUNK)
        rw[0, i] = rr_ref[:, cols]
        crv[i] = cr_ref[:, cols]
        lb[i] = jnp.broadcast_to(lab_ref[:, cols], (K_CHILD, CHUNK))

    def chunk_rows(zz):
        return pl.ds(zz * CHUNK if isinstance(zz, int) else pl.multiple_of(zz * CHUNK, CHUNK), CHUNK)

    def x_chunk(half, zz):
        return xv[half, chunk_rows(zz), :]

    def x_rows(half, places):
        return jnp.concatenate([x_chunk(half, zz) for zz in places], axis=0)

    ag_w = None
    for it in range(ROOT_ITERS):
        mine = other = gram = None
        for step, group in enumerate([[2 * i, 2 * i + 1] for i in range(4)] if it == 0 else Z_GROUPS):
            places = []
            for d in group:
                if it == 0:
                    places.append(d)
                else:
                    if d:
                        ag_w[d].wait_recv()
                    places.append(z_at(-d))
            if it == 0:
                loads[step].wait()
                loads[4 + step].wait()
            w = jnp.concatenate([rw[it, zz] for zz in places], axis=1)
            high, low = parts(w)
            other = plus(other, nn(high, x_rows(1, places)))
            mine = plus(mine, nn(high, x_rows(0, places)))
            gram = plus(gram, gram3(high, low))
        if it == 0:
            load_rc.wait()
            load_cc.wait()
            pl.semaphore_wait(barrier, 1 + len(XY) + len(Z_SEND))
        rxs[it] = other
        swap = send(rxs.at[it], rxr.at[it], s_rx.at[it], r_rx.at[it], partner)
        own_g = gfr.at[it, p]
        gfr[it, p] = padded(gram)
        gcopies = [
            send(own_g, own_g, s_gf.at[it, i], r_gf.at[it, i], xy_peer(o)) for i, o in enumerate(XY)
        ]
        swap.wait_recv()
        fr[it, p] = mine + rxr[it]
        copies = [
            send(fr.at[it, p], fr.at[it, p], s_fr.at[it, i], r_fr.at[it, i], xy_peer(o))
            for i, o in enumerate(XY)
        ]
        for i in XY_ARRIVAL:
            gcopies[i].wait_recv()
        gram = gfr[it, 0]
        for q in range(1, CHIPS):
            gram = gram + gfr[it, q]
        gfs[it] = gram
        swap = send(gfs.at[it], gft.at[it], s_gt.at[it, 0], r_gt.at[it, 0], partner)
        swap.wait_recv()
        gram = gram + gft[it]
        lower = small_product(gram[:, 0:K_ROOT], rh[it, 0], K_ROOT)
        for i in XY_ARRIVAL:
            copies[i].wait_recv()
        total = fr[it, 0]
        for q in range(1, CHIPS):
            total = total + fr[it, q]
        h = rh[it, 0] * total / lower
        rh[it + 1, 0] = h
        swap = send(rh.at[it + 1, 0], rh.at[it + 1, 1], s_rh.at[it], r_rh.at[it], partner)
        high, low = parts(h)
        ghr_own[it] = padded(gram3(high, low))
        gcopies = {
            d: send(ghr_own.at[it], ghr_in.at[it, d], s_gz.at[it, d], r_gz.at[it, d], z_peer(d)) for d in Z_SEND
        }
        owns = {d: nt(high, x_chunk(0, z_at(d))) for d in Z_SEND + [0]}
        swap.wait_recv()
        high = rh[it + 1, 1].astype(BF16)
        copies = {}
        for d in Z_SEND + [0]:
            zs_r[it, d] = owns[d] + nt(high, x_chunk(1, z_at(d)))
            if d:
                copies[d] = send(zs_r.at[it, d], zr_r.at[it, d], s_zr.at[it, d], r_zr.at[it, d], z_peer(d))
        gram = ghr_own[it]
        for d in Z_ARRIVAL:
            gcopies[d].wait_recv()
            gram = gram + ghr_in[it, d]
        gzs[it] = gram
        swap = send(gzs.at[it], gzt.at[it], s_gt.at[it, 1], r_gt.at[it, 1], partner)
        swap.wait_recv()
        gram = gram + gzt[it]
        w = rw[it, z]
        lower = small_product(gram[:, 0:K_ROOT], w, K_ROOT)
        total = zs_r[it, 0]
        for d in Z_ARRIVAL:
            copies[d].wait_recv()
            total = total + zr_r[it, d]
        rw[it + 1, z] = w * total / lower
        ag_w = {
            d: send(rw.at[it + 1, z], rw.at[it + 1, z], s_rw.at[it, d], r_rw.at[it, d], z_peer(d))
            for d in Z_SEND
        }

    own16 = pl.ds(pl.multiple_of(child * K_CHILD, 16), K_CHILD)
    own8 = pl.ds(pl.multiple_of(p * 8, 8), 8)
    hb[0, 0, own16, :] = cc[...] * rh[ROOT_ITERS, 0, pl.ds(child, 1), :]

    def spread_of(zz, w):
        label = lb[zz]
        return jnp.concatenate([jnp.where(label == c, w, 0.0) for c in range(CHILDREN)], axis=0)

    lane_child = lax.div(lax.broadcasted_iota(jnp.int32, (K_CHILD, TOTAL), 1), K_CHILD)

    def diagonal(full):
        out = jnp.where(lane_child == 0, full[0:K_CHILD], 0.0)
        for c in range(1, CHILDREN):
            out = out + jnp.where(lane_child == c, full[c * K_CHILD : (c + 1) * K_CHILD], 0.0)
        return out

    for it in range(CHILD_ITERS):
        for group in Z_GROUPS:
            places, ws, spreads = [], [], []
            for d in group:
                zz = z_at(-d)
                if d:
                    ag_w[d].wait_recv()
                if it == 0:
                    label = lb[zz, 0:K_ROOT]
                    ids = lax.broadcasted_iota(jnp.int32, (K_ROOT, CHUNK), 0)
                    own_weight = jnp.sum(
                        jnp.where(label == ids, rw[ROOT_ITERS, zz], 0.0), axis=0, keepdims=True
                    )
                    w = crv[zz] * own_weight
                    cw[0, zz] = w
                else:
                    w = cw[it, zz]
                places.append(zz)
                ws.append(w)
                spreads.append(spread_of(zz, w))
            high, low = parts(jnp.concatenate(spreads, axis=1))
            w = jnp.concatenate(ws, axis=1)
            first, last = group is Z_GROUPS[0], group is Z_GROUPS[-1]
            numer = nn(high, x_rows(1, places))
            nps[it] = numer if first else nps[it] + numer
            if last:
                swap = send(nps.at[it], cxr.at[it], s_cx.at[it, 0], r_cx.at[it, 0], partner)
            gram = nt(jnp.concatenate([high, low], axis=0), jnp.concatenate(parts(w), axis=0))
            gram = gram if first else gacc[...] + gram
            if not last:
                gacc[...] = gram
            else:
                gcs[it] = padded(
                    gram[0:TOTAL, 0:K_CHILD] + (gram[0:TOTAL, K_CHILD:] + gram[TOTAL:, 0:K_CHILD])
                )
                gcopies = []
                for i, o in enumerate(XY):
                    rows = pl.ds(pl.multiple_of(chip(*o) * 8, 8), 8)
                    gcopies.append(
                        send(gcs.at[it, rows], gcr.at[it, i], s_gc.at[it, i], r_gc.at[it, i], xy_peer(o))
                    )
            numer = nn(high, x_rows(0, places))
            no[...] = numer if first else no[...] + numer
        swap.wait_recv()
        copies = []
        for i, o in enumerate(XY):
            q = chip(*o)
            rows = pl.ds(pl.multiple_of(q * 8, 8), 8)
            rss[it, q] = no[rows, :] + cxr[it, rows, :]
            copies.append(send(rss.at[it, q], rsr.at[it, i], s_rs.at[it, i], r_rs.at[it, i], xy_peer(o)))
        total = no[own8, :] + cxr[it, own8, :]
        gram = gcs[it, own8, :]
        for i in XY_ARRIVAL:
            gcopies[i].wait_recv()
            gram = gram + gcr[it, i]
        gxs[it, 0] = gram
        swap_g = send(gxs.at[it, 0], gxr.at[it, 0], s_cx.at[it, 1], r_cx.at[it, 1], partner)
        swap_g.wait_recv()
        gram = gram + gxr[it, 0]
        old16 = hb[it, 0, own16, :]
        lower = small_product(gram[:, 0:K_CHILD], old16, K_CHILD)
        for i in XY_ARRIVAL:
            copies[i].wait_recv()
            total = total + rsr[it, i]
        hb[it + 1, 0, own8, :] = hb[it, 0, own8, :] * total / lower
        own_h = hb.at[it + 1, 0, own8]
        copies = [
            send(own_h, own_h, s_ag.at[it, i], r_ag.at[it, i], xy_peer(o)) for i, o in enumerate(XY)
        ]
        relays = [send(own_h, hb.at[it + 1, 1, own8], s_re.at[it, 15], r_re.at[it, 15], partner)]
        for i in XY_ARRIVAL:
            copies[i].wait_recv()
            dx, dy = XY[i]
            rows = pl.ds(pl.multiple_of(chip(-dx, -dy) * 8, 8), 8)
            relays.append(
                send(hb.at[it + 1, 0, rows], hb.at[it + 1, 1, rows], s_re.at[it, i], r_re.at[it, i], partner)
            )
        high, low = parts(hb[it + 1, 0])
        hbb[0] = high
        full = nt(jnp.concatenate([high, low], axis=0), high)
        ghs[it] = diagonal(full[0:TOTAL] + (full[TOTAL:] + full[TOTAL:].T))
        gcopies = {
            d: send(ghs.at[it], ghr.at[it, d], s_gh.at[it, d], r_gh.at[it, d], z_peer(d)) for d in Z_SEND
        }
        for d in Z_SEND + [0]:
            acc[d] = nt(hbb[0], x_chunk(0, z_at(d)))
        for relay in relays:
            relay.wait_recv()
        hbb[1] = hb[it + 1, 1].astype(BF16)
        copies = {}
        for d in Z_SEND + [0]:
            zz = z_at(d)
            label = lb[zz]
            rows_all = acc[d] + nt(hbb[1], x_chunk(1, zz))
            numer = jnp.where(label == 0, rows_all[0:K_CHILD], 0.0)
            for c in range(1, CHILDREN):
                numer = numer + jnp.where(label == c, rows_all[c * K_CHILD : (c + 1) * K_CHILD], 0.0)
            zs_c[it, d] = numer
            if d:
                copies[d] = send(zs_c.at[it, d], zr_c.at[it, d], s_zc.at[it, d], r_zc.at[it, d], z_peer(d))
        gram = ghs[it]
        for d in Z_ARRIVAL:
            gcopies[d].wait_recv()
            gram = gram + ghr[it, d]
        gxs[it, 1:3] = gram.reshape(2, 8, TOTAL)
        swap_g = send(gxs.at[it, 1:3], gxr.at[it, 1:3], s_gx.at[it], r_gx.at[it], partner)
        w = cw[it, z]
        s_high, s_low = parts(spread_of(z, w))
        swap_g.wait_recv()
        g_high, g_low = parts(gram + gxr[it, 1:3].reshape(K_CHILD, TOTAL))
        lower = nn(g_high, s_high) + (nn(g_high, s_low) + nn(g_low, s_high))
        total = zs_c[it, 0]
        for d in Z_ARRIVAL:
            copies[d].wait_recv()
            total = total + zr_c[it, d]
        cw[it + 1, z] = w * total / lower
        ag_w = {
            d: send(cw.at[it + 1, z], cw.at[it + 1, z], s_cw.at[it, d], r_cw.at[it, d], z_peer(d))
            for d in Z_SEND
        }

    outs = []

    def put(src, dst):
        copy = pltpu.make_async_copy(src, dst, out_sem.at[len(outs)])
        copy.start()
        outs.append(copy)

    put(hb.at[CHILD_ITERS, 0], o_ch.at[:, own_cols])
    put(hb.at[CHILD_ITERS, 1], o_ch.at[:, other_cols])
    put(rh.at[ROOT_ITERS, 0], o_rh.at[:, own_cols])
    put(rh.at[ROOT_ITERS, 1], o_rh.at[:, other_cols])
    for i in range(ZN):
        put(rw.at[ROOT_ITERS, i], o_rw.at[:, i * CHUNK : (i + 1) * CHUNK])
    put(cw.at[CHILD_ITERS, z], o_cw.at[:, chunk_rows(z)])
    flush()
    for d in Z_ARRIVAL:
        ag_w[d].wait_recv()
        put(cw.at[CHILD_ITERS, z_at(-d)], o_cw.at[:, chunk_rows(z_at(-d))])
    for out in outs:
        out.wait()


def put_out(*refs):
    sources, targets, held, sem = refs[:4], refs[4:8], refs[8:12], refs[12]
    loads = [pltpu.make_async_copy(s, h, sem.at[i]) for i, (s, h) in enumerate(zip(sources, held))]
    stores = [pltpu.make_async_copy(h, t, sem.at[4 + i]) for i, (h, t) in enumerate(zip(held, targets))]
    for load in loads:
        load.start()
    for load, store in zip(loads, stores):
        load.wait()
        store.start()
    for store in stores:
        store.wait()


def body(matrix, labels, root_rows, root_cols, child_rows, child_cols):
    vmem = pl.BlockSpec(memory_space=pltpu.VMEM)
    hbm = pl.BlockSpec(memory_space=pl.ANY)
    dma = pltpu.SemaphoreType.DMA
    r, c = ROOT_ITERS, CHILD_ITERS
    n = len(XY)

    def v(*shape, dtype=F32):
        return pltpu.VMEM(shape, dtype)

    scratch = [
        v(2, NODES, HALF, dtype=BF16), v(K_CHILD, HALF), v(ZN, K_CHILD, CHUNK, dtype=jnp.int32),
        v(ZN, K_CHILD, CHUNK), v(r + 1, 2, K_ROOT, HALF), v(r + 1, ZN, K_ROOT, CHUNK),
        v(c + 1, ZN, K_CHILD, CHUNK), v(c + 1, 2, TOTAL, HALF), v(2, TOTAL, HALF, dtype=BF16),
        v(ZN, TOTAL, CHUNK), v(TOTAL, HALF), v(2 * TOTAL, 2 * K_CHILD),
        v(r, K_ROOT, HALF), v(r, K_ROOT, HALF), v(r, CHIPS, K_ROOT, HALF),
        v(r, CHIPS, K_ROOT, 128), v(r, K_ROOT, 128), v(r, K_ROOT, 128),
        v(r, K_ROOT, 128), v(r, ZN, K_ROOT, 128), v(r, K_ROOT, 128), v(r, K_ROOT, 128),
        v(r, ZN, K_ROOT, CHUNK), v(r, ZN, K_ROOT, CHUNK),
        v(c, TOTAL, HALF), v(c, TOTAL, HALF), v(c, 3, 8, TOTAL), v(c, 3, 8, TOTAL),
        v(c, CHIPS, 8, HALF), v(c, n, 8, HALF),
        v(c, ZN, K_CHILD, CHUNK), v(c, ZN, K_CHILD, CHUNK),
        v(c, TOTAL, 128), v(c, n, 8, 128), v(c, K_CHILD, TOTAL), v(c, ZN, K_CHILD, TOTAL),
        dma((10,)), dma((20,)),
        dma((r,)), dma((r,)), dma((r, n)), dma((r, n)), dma((r,)), dma((r,)),
        dma((r, ZN)), dma((r, ZN)), dma((r, ZN)), dma((r, ZN)),
        dma((c, 2)), dma((c, 2)), dma((c, n)), dma((c, n)), dma((c, n)), dma((c, n)),
        dma((c, n + 1)), dma((c, n + 1)), dma((c, ZN)), dma((c, ZN)), dma((c, ZN)), dma((c, ZN)),
        dma((c, n)), dma((c, n)), dma((c, ZN)), dma((c, ZN)), dma((c,)), dma((c,)),
        dma((r, n)), dma((r, n)), dma((r, 2)), dma((r, 2)), dma((r, ZN)), dma((r, ZN)),
    ]
    shapes = (
        jax.ShapeDtypeStruct((K_ROOT, NODES), F32),
        jax.ShapeDtypeStruct((K_ROOT, BINS), F32),
        jax.ShapeDtypeStruct((K_CHILD, NODES), F32),
        jax.ShapeDtypeStruct((TOTAL, BINS), F32),
    )
    outs = pl.pallas_call(
        kernel,
        out_shape=shapes,
        in_specs=[hbm, vmem, vmem, hbm, vmem, hbm],
        out_specs=(hbm,) * 4,
        scratch_shapes=scratch,
        compiler_params=pltpu.CompilerParams(
            collective_id=0, has_side_effects=True, vmem_limit_bytes=63 * 1024 * 1024
        ),
        name="nmf",
    )(matrix, labels.reshape(1, NODES), root_rows, root_cols, child_rows, child_cols)
    return pl.pallas_call(
        put_out,
        out_shape=shapes,
        in_specs=[hbm] * 4,
        out_specs=(hbm,) * 4,
        scratch_shapes=[v(*s.shape) for s in shapes] + [dma((8,))],
        compiler_params=pltpu.CompilerParams(vmem_limit_bytes=63 * 1024 * 1024),
        name="put_out",
    )(*outs)


def solution(mesh):
    return jax.shard_map(
        body,
        mesh=mesh,
        in_specs=(
            P("row", "col"), P("row", None), P(None, "row"),
            P(None, "col"), P(None, "row"), P(None, "col"),
        ),
        out_specs=(P(None, "row"), P(None, "col"), P(None, "row"), P(None, "col")),
        check_vma=False,
    )
```

```python
import jax
import jax.numpy as jnp
from jax import lax
from jax.experimental import pallas as pl
from jax.experimental.pallas import tpu as pltpu
from jax.sharding import PartitionSpec as P

MESH = pl.DeviceIdType.MESH
F32, BF16 = jnp.float32, jnp.bfloat16
K_ROOT, K_CHILD, CHILDREN = 8, 16, 8
ROOT_ITERS, CHILD_ITERS = 2, 3
TOTAL = CHILDREN * K_CHILD
NODES, BINS, HALF = 2048, 1024, 512
ZN, CHUNK = 8, 256
CHIPS = 16


def ring(d, n):
    return min(d, n - d)


XY = sorted(
    [(dx, dy) for dx in range(4) for dy in range(4) if dx or dy],
    key=lambda o: -(ring(o[0], 4) + ring(o[1], 4)),
)
XY_ARRIVAL = list(reversed(range(len(XY))))
Z_SEND = [4, 3, 5, 2, 6, 1, 7]
Z_ARRIVAL = [1, 7, 2, 6, 3, 5, 4]
Z_GROUPS = [[0], [1, 7], [2, 6], [3, 5, 4]]


def nn(a, b):
    return jnp.dot(a, b, preferred_element_type=F32)


def nt(a, b):
    return lax.dot_general(a, b, (((1,), (1,)), ((), ())), preferred_element_type=F32)


def parts(a):
    high = a.astype(BF16)
    return high, (a - high.astype(F32)).astype(BF16)


def gram3(high, low):
    return nt(high, high) + (nt(high, low) + nt(low, high))


def padded(gram):
    rows, cols = gram.shape
    return jnp.concatenate([gram, jnp.zeros((rows, 128 - cols), F32)], axis=1)


def plus(a, b):
    return b if a is None else a + b


def small_product(gram, rows, count):
    total = gram[:, 0:1] * rows[0:1, :]
    for k in range(1, count):
        total = total + gram[:, k : k + 1] * rows[k : k + 1, :]
    return total


def kernel(
    x_hbm, lab_ref, rr_ref, rc_hbm, cr_ref, cc_hbm,
    o_rw, o_rh, o_cw, o_ch,
    xv, cc, lb, crv, rh, rw, cw, hb, hbb, acc, no, gacc,
    rxs, rxr, fr, gfr, gfs, gft, ghr_own, ghr_in, gzs, gzt, zs_r, zr_r,
    nps, cxr, gxs, gxr, rss, rsr, zs_c, zr_c, gcs, gcr, ghs, ghr,
    in_sem, out_sem,
    s_rx, r_rx, s_fr, r_fr, s_rh, r_rh, s_zr, r_zr, s_rw, r_rw,
    s_cx, r_cx, s_rs, r_rs, s_ag, r_ag, s_re, r_re, s_zc, r_zc, s_cw, r_cw,
    s_gc, r_gc, s_gh, r_gh, s_gx, r_gx, s_gf, r_gf, s_gt, r_gt, s_gz, r_gz,
):
    row, z = lax.axis_index("row"), lax.axis_index("col")
    p, core = lax.div(row, 2), lax.rem(row, 2)
    x, y = lax.div(p, 4), lax.rem(p, 4)
    child = lax.div(p, 2)

    def chip(dx, dy):
        return lax.rem(x + dx + 4, 4) * 4 + lax.rem(y + dy + 4, 4)

    def xy_peer(o):
        return {"row": chip(*o) * 2 + core, "col": z}

    def z_at(d):
        return lax.rem(z + d + ZN, ZN)

    def z_peer(d):
        return {"row": row, "col": z_at(d)}

    partner = {"row": p * 2 + 1 - core, "col": z}
    pending = []

    def send(src, dst, ssem, rsem, device):
        copy = pltpu.make_async_remote_copy(
            src_ref=src, dst_ref=dst, send_sem=ssem, recv_sem=rsem,
            device_id=device, device_id_type=MESH,
        )
        copy.start()
        pending.append(copy)
        return copy

    def flush():
        while pending:
            pending.pop(0).wait_send()

    loads = []
    for half in range(2):
        first = pl.multiple_of(HALF * (core if half == 0 else 1 - core), HALF)
        for i in range(4):
            rows = pl.ds(i * 512, 512)
            loads.append(
                pltpu.make_async_copy(
                    x_hbm.at[rows, pl.ds(first, HALF)], xv.at[half, rows], in_sem.at[half * 4 + i]
                )
            )
    own_cols = pl.ds(pl.multiple_of(HALF * core, HALF), HALF)
    other_cols = pl.ds(pl.multiple_of(HALF * (1 - core), HALF), HALF)
    load_cc = pltpu.make_async_copy(
        cc_hbm.at[pl.ds(pl.multiple_of(child * K_CHILD, 16), K_CHILD), own_cols], cc, in_sem.at[8]
    )
    load_rc = pltpu.make_async_copy(rc_hbm.at[:, own_cols], rh.at[0, 0], in_sem.at[9])
    for load in loads:
        load.start()
    load_rc.start()
    load_cc.start()

    barrier = pltpu.get_barrier_semaphore()
    pl.semaphore_signal(barrier, inc=1, device_id=partner, device_id_type=MESH)
    for o in XY:
        pl.semaphore_signal(barrier, inc=1, device_id=xy_peer(o), device_id_type=MESH)
    for d in Z_SEND:
        pl.semaphore_signal(barrier, inc=1, device_id=z_peer(d), device_id_type=MESH)

    for i in range(ZN):
        cols = slice(i * CHUNK, (i + 1) * CHUNK)
        rw[0, i] = rr_ref[:, cols]
        crv[i] = cr_ref[:, cols]
        lb[i] = jnp.broadcast_to(lab_ref[:, cols], (K_CHILD, CHUNK))

    def chunk_rows(zz):
        return pl.ds(zz * CHUNK if isinstance(zz, int) else pl.multiple_of(zz * CHUNK, CHUNK), CHUNK)

    def x_chunk(half, zz):
        return xv[half, chunk_rows(zz), :]

    def x_rows(half, places):
        return jnp.concatenate([x_chunk(half, zz) for zz in places], axis=0)

    ag_w = None
    for it in range(ROOT_ITERS):
        mine = other = gram = None
        for step, group in enumerate([[2 * i, 2 * i + 1] for i in range(4)] if it == 0 else Z_GROUPS):
            places = []
            for d in group:
                if it == 0:
                    places.append(d)
                else:
                    if d:
                        ag_w[d].wait_recv()
                    places.append(z_at(-d))
            if it == 0:
                loads[step].wait()
                loads[4 + step].wait()
            w = jnp.concatenate([rw[it, zz] for zz in places], axis=1)
            high, low = parts(w)
            other = plus(other, nn(high, x_rows(1, places)))
            mine = plus(mine, nn(high, x_rows(0, places)))
            gram = plus(gram, gram3(high, low))
        if it == 0:
            load_rc.wait()
            load_cc.wait()
            pl.semaphore_wait(barrier, 1 + len(XY) + len(Z_SEND))
        rxs[it] = other
        swap = send(rxs.at[it], rxr.at[it], s_rx.at[it], r_rx.at[it], partner)
        own_g = gfr.at[it, p]
        gfr[it, p] = padded(gram)
        gcopies = [
            send(own_g, own_g, s_gf.at[it, i], r_gf.at[it, i], xy_peer(o)) for i, o in enumerate(XY)
        ]
        swap.wait_recv()
        fr[it, p] = mine + rxr[it]
        copies = [
            send(fr.at[it, p], fr.at[it, p], s_fr.at[it, i], r_fr.at[it, i], xy_peer(o))
            for i, o in enumerate(XY)
        ]
        for i in XY_ARRIVAL:
            gcopies[i].wait_recv()
        gram = gfr[it, 0]
        for q in range(1, CHIPS):
            gram = gram + gfr[it, q]
        gfs[it] = gram
        swap = send(gfs.at[it], gft.at[it], s_gt.at[it, 0], r_gt.at[it, 0], partner)
        swap.wait_recv()
        gram = gram + gft[it]
        lower = small_product(gram[:, 0:K_ROOT], rh[it, 0], K_ROOT)
        for i in XY_ARRIVAL:
            copies[i].wait_recv()
        total = fr[it, 0]
        for q in range(1, CHIPS):
            total = total + fr[it, q]
        h = rh[it, 0] * total / lower
        rh[it + 1, 0] = h
        swap = send(rh.at[it + 1, 0], rh.at[it + 1, 1], s_rh.at[it], r_rh.at[it], partner)
        high, low = parts(h)
        ghr_own[it] = padded(gram3(high, low))
        gcopies = {
            d: send(ghr_own.at[it], ghr_in.at[it, d], s_gz.at[it, d], r_gz.at[it, d], z_peer(d)) for d in Z_SEND
        }
        owns = {d: nt(high, x_chunk(0, z_at(d))) for d in Z_SEND + [0]}
        swap.wait_recv()
        high = rh[it + 1, 1].astype(BF16)
        copies = {}
        for d in Z_SEND + [0]:
            zs_r[it, d] = owns[d] + nt(high, x_chunk(1, z_at(d)))
            if d:
                copies[d] = send(zs_r.at[it, d], zr_r.at[it, d], s_zr.at[it, d], r_zr.at[it, d], z_peer(d))
        gram = ghr_own[it]
        for d in Z_ARRIVAL:
            gcopies[d].wait_recv()
            gram = gram + ghr_in[it, d]
        gzs[it] = gram
        swap = send(gzs.at[it], gzt.at[it], s_gt.at[it, 1], r_gt.at[it, 1], partner)
        swap.wait_recv()
        gram = gram + gzt[it]
        w = rw[it, z]
        lower = small_product(gram[:, 0:K_ROOT], w, K_ROOT)
        total = zs_r[it, 0]
        for d in Z_ARRIVAL:
            copies[d].wait_recv()
            total = total + zr_r[it, d]
        rw[it + 1, z] = w * total / lower
        ag_w = {
            d: send(rw.at[it + 1, z], rw.at[it + 1, z], s_rw.at[it, d], r_rw.at[it, d], z_peer(d))
            for d in Z_SEND
        }

    own16 = pl.ds(pl.multiple_of(child * K_CHILD, 16), K_CHILD)
    own8 = pl.ds(pl.multiple_of(p * 8, 8), 8)
    hb[0, 0, own16, :] = cc[...] * rh[ROOT_ITERS, 0, pl.ds(child, 1), :]

    def spread_of(zz, w):
        label = lb[zz]
        return jnp.concatenate([jnp.where(label == c, w, 0.0) for c in range(CHILDREN)], axis=0)

    lane_child = lax.div(lax.broadcasted_iota(jnp.int32, (K_CHILD, TOTAL), 1), K_CHILD)

    def diagonal(full):
        out = jnp.where(lane_child == 0, full[0:K_CHILD], 0.0)
        for c in range(1, CHILDREN):
            out = out + jnp.where(lane_child == c, full[c * K_CHILD : (c + 1) * K_CHILD], 0.0)
        return out

    for it in range(CHILD_ITERS):
        for group in Z_GROUPS:
            places, ws, spreads = [], [], []
            for d in group:
                zz = z_at(-d)
                if d:
                    ag_w[d].wait_recv()
                if it == 0:
                    label = lb[zz, 0:K_ROOT]
                    ids = lax.broadcasted_iota(jnp.int32, (K_ROOT, CHUNK), 0)
                    own_weight = jnp.sum(
                        jnp.where(label == ids, rw[ROOT_ITERS, zz], 0.0), axis=0, keepdims=True
                    )
                    w = crv[zz] * own_weight
                    cw[0, zz] = w
                else:
                    w = cw[it, zz]
                places.append(zz)
                ws.append(w)
                spreads.append(spread_of(zz, w))
            high, low = parts(jnp.concatenate(spreads, axis=1))
            w = jnp.concatenate(ws, axis=1)
            first, last = group is Z_GROUPS[0], group is Z_GROUPS[-1]
            numer = nn(high, x_rows(1, places))
            nps[it] = numer if first else nps[it] + numer
            if last:
                swap = send(nps.at[it], cxr.at[it], s_cx.at[it, 0], r_cx.at[it, 0], partner)
            gram = nt(jnp.concatenate([high, low], axis=0), jnp.concatenate(parts(w), axis=0))
            gram = gram if first else gacc[...] + gram
            if not last:
                gacc[...] = gram
            else:
                gcs[it] = padded(
                    gram[0:TOTAL, 0:K_CHILD] + (gram[0:TOTAL, K_CHILD:] + gram[TOTAL:, 0:K_CHILD])
                )
                gcopies = []
                for i, o in enumerate(XY):
                    rows = pl.ds(pl.multiple_of(chip(*o) * 8, 8), 8)
                    gcopies.append(
                        send(gcs.at[it, rows], gcr.at[it, i], s_gc.at[it, i], r_gc.at[it, i], xy_peer(o))
                    )
            numer = nn(high, x_rows(0, places))
            no[...] = numer if first else no[...] + numer
        swap.wait_recv()
        copies = []
        for i, o in enumerate(XY):
            q = chip(*o)
            rows = pl.ds(pl.multiple_of(q * 8, 8), 8)
            rss[it, q] = no[rows, :] + cxr[it, rows, :]
            copies.append(send(rss.at[it, q], rsr.at[it, i], s_rs.at[it, i], r_rs.at[it, i], xy_peer(o)))
        total = no[own8, :] + cxr[it, own8, :]
        gram = gcs[it, own8, :]
        for i in XY_ARRIVAL:
            gcopies[i].wait_recv()
            gram = gram + gcr[it, i]
        gxs[it, 0] = gram
        swap_g = send(gxs.at[it, 0], gxr.at[it, 0], s_cx.at[it, 1], r_cx.at[it, 1], partner)
        swap_g.wait_recv()
        gram = gram + gxr[it, 0]
        old16 = hb[it, 0, own16, :]
        lower = small_product(gram[:, 0:K_CHILD], old16, K_CHILD)
        for i in XY_ARRIVAL:
            copies[i].wait_recv()
            total = total + rsr[it, i]
        hb[it + 1, 0, own8, :] = hb[it, 0, own8, :] * total / lower
        own_h = hb.at[it + 1, 0, own8]
        copies = [
            send(own_h, own_h, s_ag.at[it, i], r_ag.at[it, i], xy_peer(o)) for i, o in enumerate(XY)
        ]
        relays = [send(own_h, hb.at[it + 1, 1, own8], s_re.at[it, 15], r_re.at[it, 15], partner)]
        for i in XY_ARRIVAL:
            copies[i].wait_recv()
            dx, dy = XY[i]
            rows = pl.ds(pl.multiple_of(chip(-dx, -dy) * 8, 8), 8)
            relays.append(
                send(hb.at[it + 1, 0, rows], hb.at[it + 1, 1, rows], s_re.at[it, i], r_re.at[it, i], partner)
            )
        high, low = parts(hb[it + 1, 0])
        hbb[0] = high
        full = nt(jnp.concatenate([high, low], axis=0), high)
        ghs[it] = diagonal(full[0:TOTAL] + (full[TOTAL:] + full[TOTAL:].T))
        gcopies = {
            d: send(ghs.at[it], ghr.at[it, d], s_gh.at[it, d], r_gh.at[it, d], z_peer(d)) for d in Z_SEND
        }
        for d in Z_SEND + [0]:
            acc[d] = nt(hbb[0], x_chunk(0, z_at(d)))
        for relay in relays:
            relay.wait_recv()
        hbb[1] = hb[it + 1, 1].astype(BF16)
        copies = {}
        for d in Z_SEND + [0]:
            zz = z_at(d)
            label = lb[zz]
            rows_all = acc[d] + nt(hbb[1], x_chunk(1, zz))
            numer = jnp.where(label == 0, rows_all[0:K_CHILD], 0.0)
            for c in range(1, CHILDREN):
                numer = numer + jnp.where(label == c, rows_all[c * K_CHILD : (c + 1) * K_CHILD], 0.0)
            zs_c[it, d] = numer
            if d:
                copies[d] = send(zs_c.at[it, d], zr_c.at[it, d], s_zc.at[it, d], r_zc.at[it, d], z_peer(d))
        gram = ghs[it]
        for d in Z_ARRIVAL:
            gcopies[d].wait_recv()
            gram = gram + ghr[it, d]
        gxs[it, 1:3] = gram.reshape(2, 8, TOTAL)
        swap_g = send(gxs.at[it, 1:3], gxr.at[it, 1:3], s_gx.at[it], r_gx.at[it], partner)
        w = cw[it, z]
        s_high, s_low = parts(spread_of(z, w))
        swap_g.wait_recv()
        g_high, g_low = parts(gram + gxr[it, 1:3].reshape(K_CHILD, TOTAL))
        lower = nn(g_high, s_high) + (nn(g_high, s_low) + nn(g_low, s_high))
        total = zs_c[it, 0]
        for d in Z_ARRIVAL:
            copies[d].wait_recv()
            total = total + zr_c[it, d]
        cw[it + 1, z] = w * total / lower
        ag_w = {
            d: send(cw.at[it + 1, z], cw.at[it + 1, z], s_cw.at[it, d], r_cw.at[it, d], z_peer(d))
            for d in Z_SEND
        }

    outs = []

    def put(src, dst):
        copy = pltpu.make_async_copy(src, dst, out_sem.at[len(outs)])
        copy.start()
        outs.append(copy)

    put(hb.at[CHILD_ITERS, 0], o_ch.at[:, own_cols])
    put(hb.at[CHILD_ITERS, 1], o_ch.at[:, other_cols])
    put(rh.at[ROOT_ITERS, 0], o_rh.at[:, own_cols])
    put(rh.at[ROOT_ITERS, 1], o_rh.at[:, other_cols])
    for i in range(ZN):
        put(rw.at[ROOT_ITERS, i], o_rw.at[:, i * CHUNK : (i + 1) * CHUNK])
    put(cw.at[CHILD_ITERS, z], o_cw.at[:, chunk_rows(z)])
    flush()
    for d in Z_ARRIVAL:
        ag_w[d].wait_recv()
        put(cw.at[CHILD_ITERS, z_at(-d)], o_cw.at[:, chunk_rows(z_at(-d))])
    for out in outs:
        out.wait()


def put_out(*refs):
    sources, targets, held, sem = refs[:4], refs[4:8], refs[8:12], refs[12]
    pieces = [(3, slice(i * 32, (i + 1) * 32)) for i in range(4)]
    pieces += [(2, slice(0, K_CHILD)), (0, slice(0, K_ROOT)), (1, slice(0, K_ROOT))]
    loads = [
        pltpu.make_async_copy(sources[a].at[rows], held[a].at[rows], sem.at[i])
        for i, (a, rows) in enumerate(pieces)
    ]
    stores = [
        pltpu.make_async_copy(held[a].at[rows], targets[a].at[rows], sem.at[7 + i])
        for i, (a, rows) in enumerate(pieces)
    ]
    for load in loads:
        load.start()
    for load, store in zip(loads, stores):
        load.wait()
        store.start()
    for store in stores:
        store.wait()


def body(matrix, labels, root_rows, root_cols, child_rows, child_cols):
    vmem = pl.BlockSpec(memory_space=pltpu.VMEM)
    hbm = pl.BlockSpec(memory_space=pl.ANY)
    dma = pltpu.SemaphoreType.DMA
    r, c = ROOT_ITERS, CHILD_ITERS
    n = len(XY)

    def v(*shape, dtype=F32):
        return pltpu.VMEM(shape, dtype)

    scratch = [
        v(2, NODES, HALF, dtype=BF16), v(K_CHILD, HALF), v(ZN, K_CHILD, CHUNK, dtype=jnp.int32),
        v(ZN, K_CHILD, CHUNK), v(r + 1, 2, K_ROOT, HALF), v(r + 1, ZN, K_ROOT, CHUNK),
        v(c + 1, ZN, K_CHILD, CHUNK), v(c + 1, 2, TOTAL, HALF), v(2, TOTAL, HALF, dtype=BF16),
        v(ZN, TOTAL, CHUNK), v(TOTAL, HALF), v(2 * TOTAL, 2 * K_CHILD),
        v(r, K_ROOT, HALF), v(r, K_ROOT, HALF), v(r, CHIPS, K_ROOT, HALF),
        v(r, CHIPS, K_ROOT, 128), v(r, K_ROOT, 128), v(r, K_ROOT, 128),
        v(r, K_ROOT, 128), v(r, ZN, K_ROOT, 128), v(r, K_ROOT, 128), v(r, K_ROOT, 128),
        v(r, ZN, K_ROOT, CHUNK), v(r, ZN, K_ROOT, CHUNK),
        v(c, TOTAL, HALF), v(c, TOTAL, HALF), v(c, 3, 8, TOTAL), v(c, 3, 8, TOTAL),
        v(c, CHIPS, 8, HALF), v(c, n, 8, HALF),
        v(c, ZN, K_CHILD, CHUNK), v(c, ZN, K_CHILD, CHUNK),
        v(c, TOTAL, 128), v(c, n, 8, 128), v(c, K_CHILD, TOTAL), v(c, ZN, K_CHILD, TOTAL),
        dma((10,)), dma((20,)),
        dma((r,)), dma((r,)), dma((r, n)), dma((r, n)), dma((r,)), dma((r,)),
        dma((r, ZN)), dma((r, ZN)), dma((r, ZN)), dma((r, ZN)),
        dma((c, 2)), dma((c, 2)), dma((c, n)), dma((c, n)), dma((c, n)), dma((c, n)),
        dma((c, n + 1)), dma((c, n + 1)), dma((c, ZN)), dma((c, ZN)), dma((c, ZN)), dma((c, ZN)),
        dma((c, n)), dma((c, n)), dma((c, ZN)), dma((c, ZN)), dma((c,)), dma((c,)),
        dma((r, n)), dma((r, n)), dma((r, 2)), dma((r, 2)), dma((r, ZN)), dma((r, ZN)),
    ]
    shapes = (
        jax.ShapeDtypeStruct((K_ROOT, NODES), F32),
        jax.ShapeDtypeStruct((K_ROOT, BINS), F32),
        jax.ShapeDtypeStruct((K_CHILD, NODES), F32),
        jax.ShapeDtypeStruct((TOTAL, BINS), F32),
    )
    outs = pl.pallas_call(
        kernel,
        out_shape=shapes,
        in_specs=[hbm, vmem, vmem, hbm, vmem, hbm],
        out_specs=(hbm,) * 4,
        scratch_shapes=scratch,
        compiler_params=pltpu.CompilerParams(
            collective_id=0, has_side_effects=True, vmem_limit_bytes=63 * 1024 * 1024
        ),
        name="nmf",
    )(matrix, labels.reshape(1, NODES), root_rows, root_cols, child_rows, child_cols)
    return pl.pallas_call(
        put_out,
        out_shape=shapes,
        in_specs=[hbm] * 4,
        out_specs=(hbm,) * 4,
        scratch_shapes=[v(*s.shape) for s in shapes] + [dma((14,))],
        compiler_params=pltpu.CompilerParams(vmem_limit_bytes=63 * 1024 * 1024),
        name="put_out",
    )(*outs)


def solution(mesh):
    return jax.shard_map(
        body,
        mesh=mesh,
        in_specs=(
            P("row", "col"), P("row", None), P(None, "row"),
            P(None, "col"), P(None, "row"), P(None, "col"),
        ),
        out_specs=(P(None, "row"), P(None, "col"), P(None, "row"), P(None, "col")),
        check_vma=False,
    )
```
